32 devices in a mesh: pts: 8 (over y, x, core), val: 4 (over z).
Axes of the slice: x: 2, y: 2, z: 4, core: 2. Of those that a mesh axis runs over, the one named last changes fastest.
Arguments:
- trials: bfloat16 [2, 1024, 1024], P(None, 'val', 'pts'), may hold values from -6 to 6
- psi_val: bfloat16 [8192, 1024], P('pts', 'val'), may hold values from -0.1875 to 0.1875
- psi_cond: bfloat16 [8192, 1024], P('pts'), may hold values from -0.1875 to 0.1875
- kernel: bfloat16 [8192, 8192], P(None, ('pts', 'val')), may hold values from -0.5 to 0.5
- eps_val: float32 [1024], P('val'), may hold values from -1.75 to -0.25
- eps_cond: float32 [1024], replicated, may hold values from 0.5 to 1.5
Outputs:
- first: float32 [2, 1024, 1024], P(None, 'val', 'pts')
- filtered: float32 [2, 1024, 1024], P(None, 'val', 'pts')
The draws below stay inside these ranges and needn't reach their ends.
All inputs are finite; a program needn't handle non-finite values.
Results may differ from the reference program's by a relative error of at most 0.025.
Values may be sent and summed in bfloat16 or wider, within the bound.
A program may use at most 64 MiB of HBM per device.

```python
import jax
import jax.numpy as jnp
from jax import lax

NV = 1024
NC = 1024
NMU = 8192
K = 2
N_PTS = 8


def with_spikes(array, rng, source, target, blocks, factor):
    def block_of(position):
        return (jnp.arange(array.shape[position]) // (array.shape[position] // blocks)).reshape((-1,) + (1,) * (array.ndim - 1 - position))

    one_side = jax.random.permutation(rng, blocks)[block_of(target)]
    other_side = (block_of(target) + blocks // 2) % blocks
    return jnp.where((block_of(source) == one_side) | (block_of(source) == other_side), factor * array, array)


def steps_of(key, extent, shards, low, top_value):
    level = 1.0
    for dim, parts in shards:
        heights = jax.random.uniform(jax.random.fold_in(jax.random.fold_in(key, 6), dim), (parts,), jnp.float32, low / len(shards), top_value / len(shards))
        level = level * jnp.repeat(jnp.exp(heights), extent[dim] // parts).reshape((-1,) + (1,) * (len(extent) - 1 - dim))
    return level


def normal_values(stream_key, shape, width, limit, cuts=(), dtype=jnp.bfloat16):
    loudness = steps_of(stream_key, shape, cuts, -0.22, 0.18) if cuts else 1.0
    values = jax.random.normal(stream_key, shape, jnp.float32) * width * loudness
    return jnp.minimum(jnp.maximum(values, -limit), limit).astype(dtype)


def heavy_noise(stream_key, shape, scale, reach, split, heavy, held_as=jnp.bfloat16):
    drawn = scale * jax.random.normal(stream_key, shape, jnp.float32)
    if split:
        drawn = drawn * steps_of(stream_key, shape, split, -0.22, 0.18)
    return jnp.clip(with_spikes(drawn, jax.random.fold_in(stream_key, 3), *heavy), -reach, reach).astype(held_as)


def setup_inputs(seed: int = 0) -> dict:
    streams_of = jax.random.split(jax.random.key(seed), 7)
    return {
        "trials": normal_values(streams_of[0], (K, NV, NC), 1.0, 6.0, ((1, 4), (2, 8))),
        "psi_val": normal_values(streams_of[1], (NMU, NV), NV ** -0.5, 0.1875, ((0, 8), (1, 4))),
        "psi_cond": normal_values(streams_of[2], (NMU, NC), NC ** -0.5, 0.1875, ((0, 8),)),
        "kernel": heavy_noise(streams_of[3], (NMU, NMU), (NMU // 16) ** -0.5, 0.5, ((1, 32),), (1, 0, 32, 2.75)),
        "eps_val": jnp.clip(-1.75 + 1.5 * jax.random.uniform(streams_of[4], (NV,), jnp.float32) ** steps_of(streams_of[4], (NV,), ((0, 4),), -0.2, 0.2), -1.75, -0.25),
        "eps_cond": jnp.clip(jax.random.uniform(streams_of[5], (NC,), jnp.float32, 0.5, 1.5), 0.5, 1.5),
    }


center_shift = 1.75
half_width = 1.25


def apply_kernel(trial, psi_val, psi_cond, kernel):
    block_pts = NMU // N_PTS
    val_blocks = psi_val.reshape(N_PTS, block_pts, NV)
    cond_blocks = psi_cond.reshape(N_PTS, block_pts, NC)
    trial_wide = trial.astype(jnp.float32)

    def density(pieces):
        val_piece, cond_piece = pieces
        inner = jnp.einsum('kvc,mc->kvm', trial_wide, cond_piece.astype(jnp.float32))
        return jnp.einsum('mv,kvm->km', val_piece.astype(jnp.float32), inner)

    rho_blocks = lax.map(density, (val_blocks, cond_blocks))
    rho = jnp.transpose(rho_blocks, (1, 0, 2)).reshape(K, NMU).astype(jnp.bfloat16)
    image = jnp.einsum('km,nm->kn', rho.astype(jnp.float32), kernel.astype(jnp.float32))
    image_blocks = jnp.transpose(image.reshape(K, N_PTS, block_pts), (1, 0, 2))

    def accumulate(total, pieces):
        val_piece, cond_piece, image_piece = pieces
        weighted = (jnp.transpose(val_piece.astype(jnp.float32))[None] * image_piece[:, None, :]).astype(jnp.bfloat16)
        partial_sum = jnp.einsum('kvm,mc->kvc', weighted.astype(jnp.float32), cond_piece.astype(jnp.float32))
        rounded = lax.optimization_barrier(partial_sum.astype(jnp.bfloat16))
        return total + rounded.astype(jnp.float32), None

    start = jnp.zeros((K, NV, NC), jnp.float32)
    result, unused = lax.scan(accumulate, start, (val_blocks, cond_blocks, image_blocks))
    return result


def reference(trials, psi_val, psi_cond, kernel, eps_val, eps_cond):
    diff = (eps_cond[None, :] - eps_val[:, None] - center_shift)[None]
    first_image = apply_kernel(trials, psi_val, psi_cond, kernel)
    first = (diff * trials.astype(jnp.float32) + 2.0 * first_image) / half_width
    second_trial = first.astype(jnp.bfloat16)
    second_image = apply_kernel(second_trial, psi_val, psi_cond, kernel)
    filtered = 2.0 * (diff * second_trial.astype(jnp.float32) + 2.0 * second_image) / half_width - trials.astype(jnp.float32)
    return first, filtered
```

```python
import jax
import jax.numpy as jnp
from jax import lax
from jax.experimental import pallas as pl
from jax.experimental.pallas import tpu as pltpu
from jax.sharding import PartitionSpec as P

center_shift = 1.75
half_width = 1.25


def gathered_inner(local_trial, psi_cond):
    return jnp.einsum(
        "kvc,mc->kvm",
        lax.all_gather(local_trial, "pts", axis=2, tiled=True),
        psi_cond,
        preferred_element_type=jnp.float32,
    )


def orbital_terms(inner, psi_val, psi_cond, kernel):
    rho_part = jnp.einsum("mv,kvm->km", psi_val.astype(jnp.float32), inner)
    rho = lax.psum_scatter(rho_part, "val", scatter_dimension=1, tiled=True).astype(jnp.bfloat16)
    image_part = jnp.einsum("km,nm->kn", rho, kernel, preferred_element_type=jnp.float32)
    image_rows = lax.psum_scatter(
        image_part.astype(jnp.bfloat16), "pts", scatter_dimension=1, tiled=True
    ).astype(jnp.float32)
    image = lax.psum(image_rows, "val")
    weighted = (jnp.transpose(psi_val.astype(jnp.float32))[None] * image[:, None, :]).astype(
        jnp.bfloat16
    )
    return jnp.einsum("kvm,mc->kvc", weighted, psi_cond, preferred_element_type=jnp.float32)


def reduced(partial_sum):
    return lax.psum_scatter(
        partial_sum.astype(jnp.bfloat16), "pts", scatter_dimension=2, tiled=True
    ).astype(jnp.float32)


def local(trials, psi_val, psi_cond, kernel, eps_val, eps_cond):
    cols_own = trials.shape[2]
    index_pts = lax.axis_index("pts")
    diff_whole = (eps_cond[None, :] - eps_val[:, None] - center_shift)[None]
    diff_own = lax.dynamic_slice_in_dim(diff_whole, index_pts * cols_own, cols_own, 2)
    first_image = reduced(
        orbital_terms(gathered_inner(trials, psi_cond), psi_val, psi_cond, kernel)
    )
    first = (diff_own * trials.astype(jnp.float32) + 2.0 * first_image) / half_width
    second_trial = first.astype(jnp.bfloat16)
    second_inner = gathered_inner(second_trial, psi_cond)
    second_image = reduced(orbital_terms(second_inner, psi_val, psi_cond, kernel))
    filtered = 2.0 * (
        diff_own * second_trial.astype(jnp.float32) + 2.0 * second_image
    ) / half_width - trials.astype(jnp.float32)
    return (first, filtered)


F32, BF16 = jnp.float32, jnp.bfloat16
NT = (((1,), (1,)), ((), ()))


def fused_kernel(n_pts, n_val, x_hbm, pv_hbm, pc_hbm, kern_hbm, ev_hbm, ec_hbm, first_ref, filt_ref,
                 x_ref, pv, pvt, cond, kern, ev_ref, ec_ref, diff, second, xg, rs, rr, im, ir, ws, wr,
                 acc, part_out, part_in, load_sem, mate_send, mate_recv, send_sem, recv_sem):
    p = lax.axis_index("pts")
    z = lax.axis_index("val")
    n_k, rows, cols = x_ref.shape
    pts_own = pv.shape[1]
    width = rr.shape[-1]
    lanes = im.shape[-1]
    step = 256

    def flipped(q, bit):
        return q + bit - 2 * bit * lax.rem(lax.div(q, bit), 2)

    mate = flipped(p, 1)
    chips = (p, flipped(p, 2), flipped(p, 4), flipped(flipped(p, 2), 4))

    load_x = pltpu.make_async_copy(x_hbm, x_ref, load_sem.at[0])
    load_x.start()
    barrier = pltpu.get_barrier_semaphore()
    for r in range(1, n_pts):
        pl.semaphore_signal(barrier, inc=1, device_id=(lax.rem(p + r, n_pts), z), device_id_type=pl.DeviceIdType.MESH)
    for s in range(1, n_val):
        for to in (p, mate):
            pl.semaphore_signal(barrier, inc=1, device_id=(to, lax.rem(z + s, n_val)), device_id_type=pl.DeviceIdType.MESH)
    load_pv = pltpu.make_async_copy(pv_hbm, pv.at[0], load_sem.at[1])
    load_pv.start()
    load_cond = []
    for d in range(4):
        at = pl.multiple_of(chips[d] * cols, cols)
        load_cond.append(pltpu.make_async_copy(
            pc_hbm.at[:, pl.ds(at, cols)], cond.at[d // 2, 0, :, pl.ds(d % 2 * cols, cols)], load_sem.at[2 + d]))
    load_ev = pltpu.make_async_copy(ev_hbm, ev_ref, load_sem.at[6])
    load_ec = pltpu.make_async_copy(ec_hbm, ec_ref, load_sem.at[7])
    for load in (*load_cond, load_ev, load_ec):
        load.start()
    load_kern = [
        pltpu.make_async_copy(kern_hbm.at[t * pts_own:(t + 1) * pts_own], kern.at[t * pts_own:(t + 1) * pts_own],
                              load_sem.at[8 + t])
        for t in range(n_pts)]
    load_x.wait()
    pl.semaphore_wait(barrier, n_pts - 1 + 2 * (n_val - 1))

    sent = []
    live = {}

    def remote(it, k, n, src, dst, to_p, to_z):
        copy = pltpu.make_async_remote_copy(
            src_ref=src, dst_ref=dst, send_sem=send_sem.at[it, k, n], recv_sem=recv_sem.at[it, k, n],
            device_id=(to_p, to_z), device_id_type=pl.DeviceIdType.MESH)
        copy.start()
        sent.append(copy)
        live[it, k, n] = copy

    def arrived(it, k, n):
        live[it, k, n].wait_recv()

    def gather_start(it, k, x):
        for d in (3, 1, 2):
            remote(it, k, d - 1, x.at[k], xg.at[it, k, d - 1], chips[d], z)

    def to_mate(n, src, dst):
        copy = pltpu.make_async_remote_copy(
            src_ref=src, dst_ref=dst, send_sem=mate_send.at[n], recv_sem=mate_recv.at[n],
            device_id=(mate, z), device_id_type=pl.DeviceIdType.MESH)
        copy.start()
        sent.append(copy)
        return copy

    def density(it, k, jj, left, right, rho):
        block = jnp.concatenate([left, right], axis=1)
        out = []
        for b in range(2):
            for t in range(pts_own // step):
                zz = lax.dot_general(block, cond[jj, b, t * step:(t + 1) * step, :], NT, preferred_element_type=F32)
                y = zz * pvt[b, :, t * step:(t + 1) * step]
                out.append(jnp.sum(y.reshape(rows // 8, 8, step), axis=0))
        return out if rho is None else [u + w for u, w in zip(rho, out)]

    def rho_start(it, k, rho):
        row = jnp.concatenate([jnp.sum(u, axis=0, keepdims=True) for u in rho], axis=1)
        for b in range(2):
            for s in range(n_val):
                at = b * pts_own + s * width
                rs[it, k, b, s] = row[:, at:at + width]
        for s in range(n_val - 1, -1, -1):
            to = lax.rem(z + s, n_val)
            for b in range(2):
                if b or s:
                    remote(it, k, 3 + 4 * b + s, rs.at[it, k, b, to], rr.at[it, k, b, s], mate if b else p, to)

    def tiled(part):
        sub = lax.broadcasted_iota(jnp.int32, (8, lanes), 0)
        out = part[:, :lanes]
        for i in range(1, pts_own // lanes):
            out = jnp.where(sub == i, part[:, i * lanes:(i + 1) * lanes], out)
        return out

    def image_start(it, k):
        own = rs[it, k, 0, z]
        for b in range(2):
            for s in range(n_val):
                if b or s:
                    arrived(it, k, 3 + 4 * b + s)
                    own = own + rr[it, k, b, s]
        own = jnp.broadcast_to(own, (8, width)).astype(BF16)
        if it == 0 and k == 0:
            for load in load_kern:
                load.wait()
        for r in range(n_pts - 1, -1, -1):
            to = lax.rem(p + r, n_pts)
            block = kern[pl.ds(pl.multiple_of(to * pts_own, pts_own), pts_own), :]
            im[it, k, r] = tiled(lax.dot_general(own, block, NT, preferred_element_type=F32))
            if r:
                remote(it, k, 10 + r, im.at[it, k, r], ir.at[it, k, r], to, z)

    def image_sum(it, k):
        total = im[it, k, 0]
        for r in range(1, n_pts):
            arrived(it, k, 10 + r)
            total = total + ir[it, k, r]
        ws[it, k] = total
        for s in range(n_val - 1, -1, -1):
            for b in range(2):
                if b or s:
                    remote(it, k, 18 + 4 * b + s, ws.at[it, k], wr.at[it, k, b, s],
                           mate if b else p, lax.rem(z + s, n_val))

    def pairs_start(it, k):
        weighted = []
        for b in range(2):
            total = None if b else ws[it, k]
            for s in range(n_val):
                if b or s:
                    arrived(it, k, 18 + 4 * b + s)
                    total = wr[it, k, b, s] if total is None else total + wr[it, k, b, s]
            row = jnp.concatenate([total[i:i + 1] for i in range(pts_own // lanes)], axis=1)
            weighted.append((pvt[b] * row).astype(BF16))
        for jj in (1, 0):
            both = (jnp.dot(weighted[0], cond[jj, 0], preferred_element_type=F32)
                    + jnp.dot(weighted[1], cond[jj, 1], preferred_element_type=F32))
            for d in ((3, 2), (1, 0))[1 - jj]:
                tile = both[:, d % 2 * cols:(d % 2 + 1) * cols]
                if d == 0:
                    acc[k] = tile
                else:
                    part_out[it, k, d - 1] = tile.astype(BF16)
                    remote(it, k, 25 + d, part_out.at[it, k, d - 1], part_in.at[it, k, d - 1], chips[d], z)

    def pairs_end(it, k):
        value = acc[k]
        for d in (1, 2, 3):
            arrived(it, k, 25 + d)
            value = value + part_in[it, k, d - 1].astype(F32)
        return value

    def apply(it, x, use):
        every = range(n_k)
        if it == 0:
            for k in every:
                gather_start(it, k, x)
            swaps = [to_mate(0, pv_hbm, pv.at[1])]
            for d in range(4):
                at = pl.multiple_of(flipped(chips[d], 1) * cols, cols)
                swaps.append(to_mate(1 + d, pc_hbm.at[:, pl.ds(at, cols)],
                                     cond.at[d // 2, 1, :, pl.ds(d % 2 * cols, cols)]))
            for load in load_kern:
                load.start()
            load_ev.wait()
            load_ec.wait()
            diff[...] = (ec_ref[:, pl.ds(pl.multiple_of(p * cols, cols), cols)]
                         - jnp.transpose(jnp.broadcast_to(ev_ref[...], (cols, rows))) - center_shift)
            load_pv.wait()
            pvt[0] = jnp.transpose(pv[0].astype(F32))
            swaps[0].wait_recv()
            pvt[1] = jnp.transpose(pv[1].astype(F32))
            for load in load_cond:
                load.wait()
            for swap in swaps[1:]:
                swap.wait_recv()
        for k in every:
            arrived(it, k, 0)
            rho = density(it, k, 0, x[k], xg[it, k, 0], None)
            arrived(it, k, 1)
            arrived(it, k, 2)
            rho = density(it, k, 1, xg[it, k, 1], xg[it, k, 2], rho)
            rho_start(it, k, rho)
        for stage in (image_start, image_sum, pairs_start):
            for k in every:
                stage(it, k)
        for k in every:
            use(k, pairs_end(it, k))

    def to_first(k, image):
        value = (diff[...] * x_ref[k].astype(F32) + 2.0 * image) / half_width
        second[k] = value.astype(BF16)
        gather_start(1, k, second)
        first_ref[k] = value

    def to_filtered(k, image):
        filt_ref[k] = 2.0 * (diff[...] * second[k].astype(F32) + 2.0 * image) / half_width - x_ref[k].astype(F32)

    apply(0, x_ref, to_first)
    apply(1, second, to_filtered)
    for copy in sent:
        copy.wait_send()


def hand_over(a, b, a_out, b_out, sem):
    copies = [pltpu.make_async_copy(a, a_out, sem.at[0]), pltpu.make_async_copy(b, b_out, sem.at[1])]
    for copy in copies:
        copy.start()
    for copy in copies:
        copy.wait()


def fused(n_pts, n_val, trials, psi_val, psi_cond, kernel, eps_val, eps_cond):
    n_k, rows, cols = trials.shape
    points = psi_val.shape[0]
    width = kernel.shape[1]
    vmem, hbm = pl.BlockSpec(memory_space=pltpu.VMEM), pl.BlockSpec(memory_space=pl.ANY)
    tile = (n_k, rows, cols)
    image = (points // 128, 128)
    kept = pltpu.VMEM(tile, F32)
    results = pl.pallas_call(
        lambda *refs: fused_kernel(n_pts, n_val, *refs),
        out_shape=(kept, kept),
        in_specs=[hbm] * 6,
        out_specs=(vmem, vmem),
        scratch_shapes=[
            pltpu.VMEM(tile, BF16),
            pltpu.VMEM((2, points, rows), BF16),
            pltpu.VMEM((2, rows, points), F32),
            pltpu.VMEM((2, 2, points, 2 * cols), BF16),
            pltpu.VMEM(kernel.shape, BF16),
            pltpu.VMEM((1, rows), F32),
            pltpu.VMEM((1, eps_cond.shape[0]), F32),
            pltpu.VMEM((rows, cols), F32),
            pltpu.VMEM(tile, BF16),
            pltpu.VMEM((2, n_k, 3, rows, cols), BF16),
            pltpu.VMEM((2, n_k, 2, n_val, 1, width), F32),
            pltpu.VMEM((2, n_k, 2, n_val, 1, width), F32),
            pltpu.VMEM((2, n_k, n_pts) + image, F32),
            pltpu.VMEM((2, n_k, n_pts) + image, F32),
            pltpu.VMEM((2, n_k) + image, F32),
            pltpu.VMEM((2, n_k, 2, n_val) + image, F32),
            pltpu.VMEM(tile, F32),
            pltpu.VMEM((2, n_k, 3, rows, cols), BF16),
            pltpu.VMEM((2, n_k, 3, rows, cols), BF16),
            pltpu.SemaphoreType.DMA((8 + n_pts,)),
            pltpu.SemaphoreType.DMA((5,)),
            pltpu.SemaphoreType.DMA((5,)),
            pltpu.SemaphoreType.DMA((2, n_k, 29)),
            pltpu.SemaphoreType.DMA((2, n_k, 29)),
        ],
        compiler_params=pltpu.CompilerParams(
            collective_id=0, has_side_effects=True, vmem_limit_bytes=56 * 1024 * 1024),
    )(trials, psi_val, psi_cond, kernel, eps_val.reshape(1, -1), eps_cond.reshape(1, -1))
    out = jax.ShapeDtypeStruct(tile, F32)
    return pl.pallas_call(
        hand_over,
        out_shape=(out, out),
        in_specs=[hbm, hbm],
        out_specs=(hbm, hbm),
        scratch_shapes=[pltpu.SemaphoreType.DMA((2,))],
        compiler_params=pltpu.CompilerParams(vmem_limit_bytes=1024 * 1024),
    )(*results)


def solution(mesh):
    n_pts, n_val = mesh.shape["pts"], mesh.shape["val"]

    def program(trials, *rest):
        whole_lanes = trials.shape[2] % 128 == 0 and rest[0].shape[1] % 128 == 0
        if whole_lanes and trials.shape[0] == 2 and n_pts == 8 and n_val <= 4:
            return fused(n_pts, n_val, trials, *rest)
        return local(trials, *rest)

    in_specs = (
        P(None, "val", "pts"),
        P("pts", "val"),
        P("pts", None),
        P(None, ("pts", "val")),
        P("val"),
        P(),
    )
    out_specs = (P(None, "val", "pts"), P(None, "val", "pts"))
    return jax.shard_map(program, mesh=mesh, in_specs=in_specs, out_specs=out_specs, check_vma=False)
```

```python
import jax
import jax.numpy as jnp
from jax import lax
from jax.experimental import pallas as pl
from jax.experimental.pallas import tpu as pltpu
from jax.sharding import PartitionSpec as P

center_shift = 1.75
half_width = 1.25


def gathered_inner(local_trial, psi_cond):
    return jnp.einsum(
        "kvc,mc->kvm",
        lax.all_gather(local_trial, "pts", axis=2, tiled=True),
        psi_cond,
        preferred_element_type=jnp.float32,
    )


def orbital_terms(inner, psi_val, psi_cond, kernel):
    rho_part = jnp.einsum("mv,kvm->km", psi_val.astype(jnp.float32), inner)
    rho = lax.psum_scatter(rho_part, "val", scatter_dimension=1, tiled=True).astype(jnp.bfloat16)
    image_part = jnp.einsum("km,nm->kn", rho, kernel, preferred_element_type=jnp.float32)
    image_rows = lax.psum_scatter(
        image_part.astype(jnp.bfloat16), "pts", scatter_dimension=1, tiled=True
    ).astype(jnp.float32)
    image = lax.psum(image_rows, "val")
    weighted = (jnp.transpose(psi_val.astype(jnp.float32))[None] * image[:, None, :]).astype(
        jnp.bfloat16
    )
    return jnp.einsum("kvm,mc->kvc", weighted, psi_cond, preferred_element_type=jnp.float32)


def reduced(partial_sum):
    return lax.psum_scatter(
        partial_sum.astype(jnp.bfloat16), "pts", scatter_dimension=2, tiled=True
    ).astype(jnp.float32)


def local(trials, psi_val, psi_cond, kernel, eps_val, eps_cond):
    cols_own = trials.shape[2]
    index_pts = lax.axis_index("pts")
    diff_whole = (eps_cond[None, :] - eps_val[:, None] - center_shift)[None]
    diff_own = lax.dynamic_slice_in_dim(diff_whole, index_pts * cols_own, cols_own, 2)
    first_image = reduced(
        orbital_terms(gathered_inner(trials, psi_cond), psi_val, psi_cond, kernel)
    )
    first = (diff_own * trials.astype(jnp.float32) + 2.0 * first_image) / half_width
    second_trial = first.astype(jnp.bfloat16)
    second_inner = gathered_inner(second_trial, psi_cond)
    second_image = reduced(orbital_terms(second_inner, psi_val, psi_cond, kernel))
    filtered = 2.0 * (
        diff_own * second_trial.astype(jnp.float32) + 2.0 * second_image
    ) / half_width - trials.astype(jnp.float32)
    return (first, filtered)


F32, BF16 = jnp.float32, jnp.bfloat16
NT = (((1,), (1,)), ((), ()))


def fused_kernel(n_pts, n_val, x_hbm, pv_hbm, pc_hbm, kern_hbm, ev_hbm, ec_hbm, first_ref, filt_ref,
                 x_ref, pv, pvt, cond, kern, ev_ref, ec_ref, diff, second, xg, rs, rr, im, ir, ws, wr,
                 acc, part_out, part_in, load_sem, mate_send, mate_recv, send_sem, recv_sem):
    p = lax.axis_index("pts")
    z = lax.axis_index("val")
    n_k, rows, cols = x_ref.shape
    pts_own = pv.shape[1]
    width = rr.shape[-1]
    lanes = im.shape[-1]
    step = 256

    def flipped(q, bit):
        return q + bit - 2 * bit * lax.rem(lax.div(q, bit), 2)

    mate = flipped(p, 1)
    chips = (p, flipped(p, 2), flipped(p, 4), flipped(flipped(p, 2), 4))

    load_x = pltpu.make_async_copy(x_hbm, x_ref, load_sem.at[0])
    load_x.start()
    barrier = pltpu.get_barrier_semaphore()
    for r in range(1, n_pts):
        pl.semaphore_signal(barrier, inc=1, device_id=(lax.rem(p + r, n_pts), z), device_id_type=pl.DeviceIdType.MESH)
    for s in range(1, n_val):
        for to in (p, mate):
            pl.semaphore_signal(barrier, inc=1, device_id=(to, lax.rem(z + s, n_val)), device_id_type=pl.DeviceIdType.MESH)
    load_pv = pltpu.make_async_copy(pv_hbm, pv.at[0], load_sem.at[1])
    load_pv.start()
    for d in range(4):
        at = pl.multiple_of(chips[d] * cols, cols)
        pltpu.make_async_copy(
            pc_hbm.at[:, pl.ds(at, cols)], cond.at[0, d // 2, :, pl.ds(d % 2 * cols, cols)], load_sem.at[2]).start()
    load_ev = pltpu.make_async_copy(ev_hbm, ev_ref, load_sem.at[3])
    load_ec = pltpu.make_async_copy(ec_hbm, ec_ref, load_sem.at[4])
    load_ev.start()
    load_ec.start()
    load_x.wait()
    pl.semaphore_wait(barrier, n_pts - 1 + 2 * (n_val - 1))

    groups = {
        "x_near": lambda it, k: xg.at[it, k, 0],
        "x_far": lambda it, k: xg.at[it, k, 1:3],
        "rho": lambda it, k: rr.at[it, k, 1:2 * n_val],
        "image": lambda it, k: ir.at[it, k, 1:n_pts],
        "points": lambda it, k: wr.at[it, k, 1:2 * n_val],
        "pairs": lambda it, k: part_in.at[it, k],
    }
    places = {name: at for at, name in enumerate(groups)}

    def wait_for(ref, sem):
        pltpu.make_async_copy(ref, ref, sem).wait()

    def remote(it, k, group, src, dst, to_p, to_z):
        n = places[group]
        pltpu.make_async_remote_copy(
            src_ref=src, dst_ref=dst, send_sem=send_sem.at[it, k, n], recv_sem=recv_sem.at[it, k, n],
            device_id=(to_p, to_z), device_id_type=pl.DeviceIdType.MESH).start()

    def arrived(it, k, group):
        wait_for(groups[group](it, k), recv_sem.at[it, k, places[group]])

    def gather_start(it, k, x):
        for d in (3, 1, 2):
            remote(it, k, "x_near" if d == 1 else "x_far", x.at[k], xg.at[it, k, d - 1], chips[d], z)

    def to_mate(n, src, dst):
        pltpu.make_async_remote_copy(
            src_ref=src, dst_ref=dst, send_sem=mate_send.at[n], recv_sem=mate_recv.at[n],
            device_id=(mate, z), device_id_type=pl.DeviceIdType.MESH).start()

    def density(it, k, jj, left, right, rho):
        block = jnp.concatenate([left, right], axis=1)
        out = []
        for b in range(2):
            for t in range(pts_own // step):
                zz = lax.dot_general(block, cond[b, jj, t * step:(t + 1) * step, :], NT, preferred_element_type=F32)
                y = zz * pvt[b, :, t * step:(t + 1) * step]
                out.append(jnp.sum(y.reshape(rows // 8, 8, step), axis=0))
        return out if rho is None else [u + w for u, w in zip(rho, out)]

    def rho_start(it, k, rho):
        row = jnp.concatenate([jnp.sum(u, axis=0, keepdims=True) for u in rho], axis=1)
        for b in range(2):
            for s in range(n_val):
                at = b * pts_own + s * width
                rs[it, k, b, s] = row[:, at:at + width]
        for s in range(n_val - 1, -1, -1):
            to = lax.rem(z + s, n_val)
            for b in range(2):
                if b or s:
                    remote(it, k, "rho", rs.at[it, k, b, to], rr.at[it, k, n_val * b + s], mate if b else p, to)

    def tiled(part):
        sub = lax.broadcasted_iota(jnp.int32, (8, lanes), 0)
        out = part[:, :lanes]
        for i in range(1, pts_own // lanes):
            out = jnp.where(sub == i, part[:, i * lanes:(i + 1) * lanes], out)
        return out

    def image_start(it, k):
        own = rs[it, k, 0, z]
        arrived(it, k, "rho")
        for i in range(1, 2 * n_val):
            own = own + rr[it, k, i]
        own = jnp.broadcast_to(own, (8, width)).astype(BF16)
        if it == 0 and k == 0:
            wait_for(kern, load_sem.at[5])
        for r in range(n_pts - 1, -1, -1):
            to = flipped(chips[r // 2], 1) if r % 2 else chips[r // 2]
            block = kern[pl.ds(pl.multiple_of(to * pts_own, pts_own), pts_own), :]
            im[it, k, r] = tiled(lax.dot_general(own, block, NT, preferred_element_type=F32))
            if r:
                remote(it, k, "image", im.at[it, k, r], ir.at[it, k, r], to, z)

    def image_sum(it, k):
        total = im[it, k, 0]
        arrived(it, k, "image")
        for r in range(1, n_pts):
            total = total + ir[it, k, r]
        ws[it, k] = total
        for s in range(n_val - 1, -1, -1):
            for b in range(2):
                if b or s:
                    remote(it, k, "points", ws.at[it, k], wr.at[it, k, n_val * b + s],
                           mate if b else p, lax.rem(z + s, n_val))

    def pairs_start(it, k):
        weighted = []
        arrived(it, k, "points")
        for b in range(2):
            total = wr[it, k, n_val] if b else ws[it, k]
            for s in range(1, n_val):
                total = total + wr[it, k, n_val * b + s]
            row = jnp.concatenate([total[i:i + 1] for i in range(pts_own // lanes)], axis=1)
            weighted.append((pvt[b] * row).astype(BF16))
        for jj in (1, 0):
            both = (jnp.dot(weighted[0], cond[0, jj], preferred_element_type=F32)
                    + jnp.dot(weighted[1], cond[1, jj], preferred_element_type=F32))
            for d in ((3, 2), (1, 0))[1 - jj]:
                tile = both[:, d % 2 * cols:(d % 2 + 1) * cols]
                if d == 0:
                    acc[k] = tile
                else:
                    part_out[it, k, d - 1] = tile.astype(BF16)
                    remote(it, k, "pairs", part_out.at[it, k, d - 1], part_in.at[it, k, d - 1], chips[d], z)

    def pairs_end(it, k):
        value = acc[k]
        arrived(it, k, "pairs")
        for d in (1, 2, 3):
            value = value + part_in[it, k, d - 1].astype(F32)
        return value

    def apply(it, x, use):
        every = range(n_k)
        if it == 0:
            for k in every:
                gather_start(it, k, x)
            to_mate(0, pv_hbm, pv.at[1])
            for d in range(4):
                at = pl.multiple_of(flipped(chips[d], 1) * cols, cols)
                to_mate(1, pc_hbm.at[:, pl.ds(at, cols)], cond.at[1, d // 2, :, pl.ds(d % 2 * cols, cols)])
            for t in range(n_pts):
                part = pl.ds(t * pts_own, pts_own)
                pltpu.make_async_copy(kern_hbm.at[part], kern.at[part], load_sem.at[5]).start()
            load_ev.wait()
            load_ec.wait()
            diff[...] = (ec_ref[:, pl.ds(pl.multiple_of(p * cols, cols), cols)]
                         - jnp.transpose(jnp.broadcast_to(ev_ref[...], (cols, rows))) - center_shift)
            load_pv.wait()
            pvt[0] = jnp.transpose(pv[0].astype(F32))
            wait_for(pv.at[1], mate_recv.at[0])
            pvt[1] = jnp.transpose(pv[1].astype(F32))
            wait_for(cond.at[0], load_sem.at[2])
            wait_for(cond.at[1], mate_recv.at[1])
        for k in every:
            arrived(it, k, "x_near")
            rho = density(it, k, 0, x[k], xg[it, k, 0], None)
            arrived(it, k, "x_far")
            rho = density(it, k, 1, xg[it, k, 1], xg[it, k, 2], rho)
            rho_start(it, k, rho)
        for stage in (image_start, image_sum, pairs_start):
            for k in every:
                stage(it, k)
        for k in every:
            use(k, pairs_end(it, k))

    def to_first(k, image):
        value = (diff[...] * x_ref[k].astype(F32) + 2.0 * image) / half_width
        second[k] = value.astype(BF16)
        gather_start(1, k, second)
        first_ref[k] = value

    def to_filtered(k, image):
        filt_ref[k] = 2.0 * (diff[...] * second[k].astype(F32) + 2.0 * image) / half_width - x_ref[k].astype(F32)

    apply(0, x_ref, to_first)
    apply(1, second, to_filtered)
    for it in range(2):
        for k in range(n_k):
            for name, ref in groups.items():
                wait_for(ref(it, k), send_sem.at[it, k, places[name]])
    wait_for(pv.at[1], mate_send.at[0])
    wait_for(cond.at[1], mate_send.at[1])


def hand_over(a, b, a_out, b_out, sem):
    copies = [pltpu.make_async_copy(a, a_out, sem.at[0]), pltpu.make_async_copy(b, b_out, sem.at[1])]
    for copy in copies:
        copy.start()
    for copy in copies:
        copy.wait()


def fused(n_pts, n_val, trials, psi_val, psi_cond, kernel, eps_val, eps_cond):
    n_k, rows, cols = trials.shape
    points = psi_val.shape[0]
    width = kernel.shape[1]
    vmem, hbm = pl.BlockSpec(memory_space=pltpu.VMEM), pl.BlockSpec(memory_space=pl.ANY)
    tile = (n_k, rows, cols)
    image = (points // 128, 128)
    kept = pltpu.VMEM(tile, F32)
    results = pl.pallas_call(
        lambda *refs: fused_kernel(n_pts, n_val, *refs),
        out_shape=(kept, kept),
        in_specs=[hbm] * 6,
        out_specs=(vmem, vmem),
        scratch_shapes=[
            pltpu.VMEM(tile, BF16),
            pltpu.VMEM((2, points, rows), BF16),
            pltpu.VMEM((2, rows, points), F32),
            pltpu.VMEM((2, 2, points, 2 * cols), BF16),
            pltpu.VMEM(kernel.shape, BF16),
            pltpu.VMEM((1, rows), F32),
            pltpu.VMEM((1, eps_cond.shape[0]), F32),
            pltpu.VMEM((rows, cols), F32),
            pltpu.VMEM(tile, BF16),
            pltpu.VMEM((2, n_k, 3, rows, cols), BF16),
            pltpu.VMEM((2, n_k, 2, n_val, 1, width), F32),
            pltpu.VMEM((2, n_k, 2 * n_val, 1, width), F32),
            pltpu.VMEM((2, n_k, n_pts) + image, F32),
            pltpu.VMEM((2, n_k, n_pts) + image, F32),
            pltpu.VMEM((2, n_k) + image, F32),
            pltpu.VMEM((2, n_k, 2 * n_val) + image, F32),
            pltpu.VMEM(tile, F32),
            pltpu.VMEM((2, n_k, 3, rows, cols), BF16),
            pltpu.VMEM((2, n_k, 3, rows, cols), BF16),
            pltpu.SemaphoreType.DMA((6,)),
            pltpu.SemaphoreType.DMA((2,)),
            pltpu.SemaphoreType.DMA((2,)),
            pltpu.SemaphoreType.DMA((2, n_k, 6)),
            pltpu.SemaphoreType.DMA((2, n_k, 6)),
        ],
        compiler_params=pltpu.CompilerParams(
            collective_id=0, has_side_effects=True, vmem_limit_bytes=56 * 1024 * 1024),
    )(trials, psi_val, psi_cond, kernel, eps_val.reshape(1, -1), eps_cond.reshape(1, -1))
    out = jax.ShapeDtypeStruct(tile, F32)
    return pl.pallas_call(
        hand_over,
        out_shape=(out, out),
        in_specs=[hbm, hbm],
        out_specs=(hbm, hbm),
        scratch_shapes=[pltpu.SemaphoreType.DMA((2,))],
        compiler_params=pltpu.CompilerParams(vmem_limit_bytes=1024 * 1024),
    )(*results)


def solution(mesh):
    n_pts, n_val = mesh.shape["pts"], mesh.shape["val"]

    def program(trials, *rest):
        whole_lanes = trials.shape[2] % 128 == 0 and rest[0].shape[1] % 128 == 0
        if whole_lanes and trials.shape[0] == 2 and n_pts == 8 and n_val <= 4:
            return fused(n_pts, n_val, trials, *rest)
        return local(trials, *rest)

    in_specs = (
        P(None, "val", "pts"),
        P("pts", "val"),
        P("pts", None),
        P(None, ("pts", "val")),
        P("val"),
        P(),
    )
    out_specs = (P(None, "val", "pts"), P(None, "val", "pts"))
    return jax.shard_map(program, mesh=mesh, in_specs=in_specs, out_specs=out_specs, check_vma=False)
```

```python
import jax
import jax.numpy as jnp
from jax import lax
from jax.experimental import pallas as pl
from jax.experimental.pallas import tpu as pltpu
from jax.sharding import PartitionSpec as P

center_shift = 1.75
half_width = 1.25


def gathered_inner(local_trial, psi_cond):
    return jnp.einsum(
        "kvc,mc->kvm",
        lax.all_gather(local_trial, "pts", axis=2, tiled=True),
        psi_cond,
        preferred_element_type=jnp.float32,
    )


def orbital_terms(inner, psi_val, psi_cond, kernel):
    rho_part = jnp.einsum("mv,kvm->km", psi_val.astype(jnp.float32), inner)
    rho = lax.psum_scatter(rho_part, "val", scatter_dimension=1, tiled=True).astype(jnp.bfloat16)
    image_part = jnp.einsum("km,nm->kn", rho, kernel, preferred_element_type=jnp.float32)
    image_rows = lax.psum_scatter(
        image_part.astype(jnp.bfloat16), "pts", scatter_dimension=1, tiled=True
    ).astype(jnp.float32)
    image = lax.psum(image_rows, "val")
    weighted = (jnp.transpose(psi_val.astype(jnp.float32))[None] * image[:, None, :]).astype(
        jnp.bfloat16
    )
    return jnp.einsum("kvm,mc->kvc", weighted, psi_cond, preferred_element_type=jnp.float32)


def reduced(partial_sum):
    return lax.psum_scatter(
        partial_sum.astype(jnp.bfloat16), "pts", scatter_dimension=2, tiled=True
    ).astype(jnp.float32)


def local(trials, psi_val, psi_cond, kernel, eps_val, eps_cond):
    cols_own = trials.shape[2]
    index_pts = lax.axis_index("pts")
    diff_whole = (eps_cond[None, :] - eps_val[:, None] - center_shift)[None]
    diff_own = lax.dynamic_slice_in_dim(diff_whole, index_pts * cols_own, cols_own, 2)
    first_image = reduced(
        orbital_terms(gathered_inner(trials, psi_cond), psi_val, psi_cond, kernel)
    )
    first = (diff_own * trials.astype(jnp.float32) + 2.0 * first_image) / half_width
    second_trial = first.astype(jnp.bfloat16)
    second_inner = gathered_inner(second_trial, psi_cond)
    second_image = reduced(orbital_terms(second_inner, psi_val, psi_cond, kernel))
    filtered = 2.0 * (
        diff_own * second_trial.astype(jnp.float32) + 2.0 * second_image
    ) / half_width - trials.astype(jnp.float32)
    return (first, filtered)


F32, BF16 = jnp.float32, jnp.bfloat16
NT = (((1,), (1,)), ((), ()))


def fused_kernel(n_pts, n_val, x_hbm, pv_hbm, pc_hbm, kern_hbm, ev_hbm, ec_hbm, first_ref, filt_ref,
                 x_ref, pv, pvt, cond, kern, kern_t, ev_ref, ec_ref, diff, second, xg, rs, rr, im, ir,
                 acc, part_out, part_in, load_sem, mate_send, mate_recv, send_sem, recv_sem):
    p = lax.axis_index("pts")
    z = lax.axis_index("val")
    n_k, rows, cols = x_ref.shape
    pts_own = pv.shape[1]
    width = rr.shape[-1] // 2
    lanes = im.shape[-1]
    step = 256

    def flipped(q, bit):
        return q + bit - 2 * bit * lax.rem(lax.div(q, bit), 2)

    mate = flipped(p, 1)
    chips = (p, flipped(p, 2), flipped(p, 4), flipped(flipped(p, 2), 4))

    load_x = pltpu.make_async_copy(x_hbm, x_ref, load_sem.at[0])
    load_x.start()
    barrier = pltpu.get_barrier_semaphore()
    for to in (*chips[1:], mate):
        pl.semaphore_signal(barrier, inc=1, device_id=(to, z), device_id_type=pl.DeviceIdType.MESH)
    for s in range(1, n_val):
        for to in (p, mate):
            pl.semaphore_signal(barrier, inc=1, device_id=(to, lax.rem(z + s, n_val)), device_id_type=pl.DeviceIdType.MESH)
    load_pv = pltpu.make_async_copy(pv_hbm, pv.at[0], load_sem.at[1])
    load_pv.start()
    for d in range(4):
        at = pl.multiple_of(chips[d] * cols, cols)
        pltpu.make_async_copy(
            pc_hbm.at[:, pl.ds(at, cols)], cond.at[0, d // 2, :, pl.ds(d % 2 * cols, cols)], load_sem.at[2]).start()
    load_ev = pltpu.make_async_copy(ev_hbm, ev_ref, load_sem.at[3])
    load_ec = pltpu.make_async_copy(ec_hbm, ec_ref, load_sem.at[4])
    load_ev.start()
    load_ec.start()
    load_x.wait()
    pl.semaphore_wait(barrier, 4 + 2 * (n_val - 1))

    groups = {
        "x_near": lambda it, k: xg.at[it, k, 0],
        "x_far": lambda it, k: xg.at[it, k, 1:3],
        "rho": lambda it, k: rr.at[it, k, 1:2 * n_val],
        "image": lambda it, k: ir.at[it, k, 1:],
        "pairs": lambda it, k: part_in.at[it, k],
    }
    places = {name: at for at, name in enumerate(groups)}

    def wait_for(ref, sem):
        pltpu.make_async_copy(ref, ref, sem).wait()

    def remote(it, k, group, src, dst, to_p, to_z):
        n = places[group]
        pltpu.make_async_remote_copy(
            src_ref=src, dst_ref=dst, send_sem=send_sem.at[it, k, n], recv_sem=recv_sem.at[it, k, n],
            device_id=(to_p, to_z), device_id_type=pl.DeviceIdType.MESH).start()

    def arrived(it, k, group):
        wait_for(groups[group](it, k), recv_sem.at[it, k, places[group]])

    def gather_start(it, k, x):
        for d in (3, 1, 2):
            remote(it, k, "x_near" if d == 1 else "x_far", x.at[k], xg.at[it, k, d - 1], chips[d], z)

    def to_mate(n, src, dst):
        pltpu.make_async_remote_copy(
            src_ref=src, dst_ref=dst, send_sem=mate_send.at[n], recv_sem=mate_recv.at[n],
            device_id=(mate, z), device_id_type=pl.DeviceIdType.MESH).start()

    def density(it, k, jj, left, right, rho):
        block = jnp.concatenate([left, right], axis=1)
        out = []
        for b in range(2):
            for t in range(pts_own // step):
                zz = lax.dot_general(block, cond[b, jj, t * step:(t + 1) * step, :], NT, preferred_element_type=F32)
                y = zz * pvt[b, :, t * step:(t + 1) * step]
                out.append(jnp.sum(y.reshape(rows // 8, 8, step), axis=0))
        return out if rho is None else [u + w for u, w in zip(rho, out)]

    def rho_start(it, k, rho):
        row = jnp.concatenate([jnp.sum(u, axis=0, keepdims=True) for u in rho], axis=1)
        for s in range(n_val):
            for b in range(2):
                tile = row[:, b * pts_own + s * width:b * pts_own + (s + 1) * width]
                rs[it, k, 0, s, :, b * width:(b + 1) * width] = tile
                rs[it, k, 1, s, :, (1 - b) * width:(2 - b) * width] = tile
        for s in range(n_val - 1, -1, -1):
            to = lax.rem(z + s, n_val)
            for b in range(2):
                if b or s:
                    remote(it, k, "rho", rs.at[it, k, b, to], rr.at[it, k, n_val * b + s], mate if b else p, to)

    def tiled(part):
        sub = lax.broadcasted_iota(jnp.int32, (8, lanes), 0)
        out = part[:, :lanes]
        for i in range(1, pts_own // lanes):
            out = jnp.where(sub == i, part[:, i * lanes:(i + 1) * lanes], out)
        return out

    def image_start(it, k):
        own = rs[it, k, 0, z]
        arrived(it, k, "rho")
        for i in range(1, 2 * n_val):
            own = own + rr[it, k, i]
        own = jnp.broadcast_to(own, (8, 2 * width)).astype(BF16)
        for d in (3, 2, 1, 0):
            part = tiled(jnp.dot(own, kern_t[d], preferred_element_type=F32))
            im[it, k, d] = part
            if d == 0:
                ir[it, k, 0] = part
            for s in range(n_val - 1, -1, -1):
                for b in range(2):
                    if b or s or d:
                        remote(it, k, "image", im.at[it, k, d], ir.at[it, k, (n_val * b + s) * 4 + d],
                               flipped(chips[d], 1) if b else chips[d], lax.rem(z + s, n_val))

    def pairs_start(it, k):
        weighted = []
        arrived(it, k, "image")
        for b in range(2):
            total = ir[it, k, 4 * n_val * b]
            for i in range(1, 4 * n_val):
                total = total + ir[it, k, 4 * n_val * b + i]
            row = jnp.concatenate([total[i:i + 1] for i in range(pts_own // lanes)], axis=1)
            weighted.append((pvt[b] * row).astype(BF16))
        for jj in (1, 0):
            both = (jnp.dot(weighted[0], cond[0, jj], preferred_element_type=F32)
                    + jnp.dot(weighted[1], cond[1, jj], preferred_element_type=F32))
            for d in ((3, 2), (1, 0))[1 - jj]:
                tile = both[:, d % 2 * cols:(d % 2 + 1) * cols]
                if d == 0:
                    acc[k] = tile
                else:
                    part_out[it, k, d - 1] = tile.astype(BF16)
                    remote(it, k, "pairs", part_out.at[it, k, d - 1], part_in.at[it, k, d - 1], chips[d], z)

    def pairs_end(it, k):
        value = acc[k]
        arrived(it, k, "pairs")
        for d in (1, 2, 3):
            value = value + part_in[it, k, d - 1].astype(F32)
        return value

    def apply(it, x, use):
        every = range(n_k)
        if it == 0:
            for k in every:
                gather_start(it, k, x)
            to_mate(0, pv_hbm, pv.at[1])
            for d in range(4):
                at = pl.multiple_of(flipped(chips[d], 1) * cols, cols)
                to_mate(1, pc_hbm.at[:, pl.ds(at, cols)], cond.at[1, d // 2, :, pl.ds(d % 2 * cols, cols)])
            for d in range(4):
                part = pl.ds(pl.multiple_of(flipped(chips[d], 1) * pts_own, pts_own), pts_own)
                to_mate(2, kern_hbm.at[part], kern.at[1, d])
            for d in range(4):
                part = pl.ds(pl.multiple_of(chips[d] * pts_own, pts_own), pts_own)
                pltpu.make_async_copy(kern_hbm.at[part], kern.at[0, d], load_sem.at[5]).start()
            load_ev.wait()
            load_ec.wait()
            diff[...] = (ec_ref[:, pl.ds(pl.multiple_of(p * cols, cols), cols)]
                         - jnp.transpose(jnp.broadcast_to(ev_ref[...], (cols, rows))) - center_shift)
            load_pv.wait()
            pvt[0] = jnp.transpose(pv[0].astype(F32))
            wait_for(pv.at[1], mate_recv.at[0])
            pvt[1] = jnp.transpose(pv[1].astype(F32))
            wait_for(cond.at[0], load_sem.at[2])
            wait_for(cond.at[1], mate_recv.at[1])
        for k in every:
            arrived(it, k, "x_near")
            rho = density(it, k, 0, x[k], xg[it, k, 0], None)
            arrived(it, k, "x_far")
            rho = density(it, k, 1, xg[it, k, 1], xg[it, k, 2], rho)
            rho_start(it, k, rho)
        if it == 0:
            for b in range(2):
                wait_for(kern.at[b], mate_recv.at[2] if b else load_sem.at[5])
                for d in range(4):
                    kern_t[d, b * width:(b + 1) * width] = jnp.transpose(kern[b, d])
        for stage in (image_start, pairs_start):
            for k in every:
                stage(it, k)
        for k in every:
            use(k, pairs_end(it, k))

    def to_first(k, image):
        value = (diff[...] * x_ref[k].astype(F32) + 2.0 * image) / half_width
        second[k] = value.astype(BF16)
        gather_start(1, k, second)
        first_ref[k] = value

    def to_filtered(k, image):
        filt_ref[k] = 2.0 * (diff[...] * second[k].astype(F32) + 2.0 * image) / half_width - x_ref[k].astype(F32)

    apply(0, x_ref, to_first)
    apply(1, second, to_filtered)
    for it in range(2):
        for k in range(n_k):
            for name, ref in groups.items():
                wait_for(ref(it, k), send_sem.at[it, k, places[name]])
    wait_for(pv.at[1], mate_send.at[0])
    wait_for(cond.at[1], mate_send.at[1])
    wait_for(kern.at[1], mate_send.at[2])


def hand_over(a, b, a_out, b_out, sem):
    copies = [pltpu.make_async_copy(a, a_out, sem.at[0]), pltpu.make_async_copy(b, b_out, sem.at[1])]
    for copy in copies:
        copy.start()
    for copy in copies:
        copy.wait()


def fused(n_pts, n_val, trials, psi_val, psi_cond, kernel, eps_val, eps_cond):
    n_k, rows, cols = trials.shape
    points = psi_val.shape[0]
    width = kernel.shape[1]
    vmem, hbm = pl.BlockSpec(memory_space=pltpu.VMEM), pl.BlockSpec(memory_space=pl.ANY)
    tile = (n_k, rows, cols)
    image = (points // 128, 128)
    kept = pltpu.VMEM(tile, F32)
    results = pl.pallas_call(
        lambda *refs: fused_kernel(n_pts, n_val, *refs),
        out_shape=(kept, kept),
        in_specs=[hbm] * 6,
        out_specs=(vmem, vmem),
        scratch_shapes=[
            pltpu.VMEM(tile, BF16),
            pltpu.VMEM((2, points, rows), BF16),
            pltpu.VMEM((2, rows, points), F32),
            pltpu.VMEM((2, 2, points, 2 * cols), BF16),
            pltpu.VMEM((2, 4, points, width), BF16),
            pltpu.VMEM((4, 2 * width, points), BF16),
            pltpu.VMEM((1, rows), F32),
            pltpu.VMEM((1, eps_cond.shape[0]), F32),
            pltpu.VMEM((rows, cols), F32),
            pltpu.VMEM(tile, BF16),
            pltpu.VMEM((2, n_k, 3, rows, cols), BF16),
            pltpu.VMEM((2, n_k, 2, n_val, 1, 2 * width), F32),
            pltpu.VMEM((2, n_k, 2 * n_val, 1, 2 * width), F32),
            pltpu.VMEM((2, n_k, 4) + image, F32),
            pltpu.VMEM((2, n_k, 8 * n_val) + image, F32),
            pltpu.VMEM(tile, F32),
            pltpu.VMEM((2, n_k, 3, rows, cols), BF16),
            pltpu.VMEM((2, n_k, 3, rows, cols), BF16),
            pltpu.SemaphoreType.DMA((6,)),
            pltpu.SemaphoreType.DMA((3,)),
            pltpu.SemaphoreType.DMA((3,)),
            pltpu.SemaphoreType.DMA((2, n_k, 5)),
            pltpu.SemaphoreType.DMA((2, n_k, 5)),
        ],
        compiler_params=pltpu.CompilerParams(
            collective_id=0, has_side_effects=True, vmem_limit_bytes=56 * 1024 * 1024),
    )(trials, psi_val, psi_cond, kernel, eps_val.reshape(1, -1), eps_cond.reshape(1, -1))
    out = jax.ShapeDtypeStruct(tile, F32)
    return pl.pallas_call(
        hand_over,
        out_shape=(out, out),
        in_specs=[hbm, hbm],
        out_specs=(hbm, hbm),
        scratch_shapes=[pltpu.SemaphoreType.DMA((2,))],
        compiler_params=pltpu.CompilerParams(vmem_limit_bytes=1024 * 1024),
    )(*results)


def solution(mesh):
    n_pts, n_val = mesh.shape["pts"], mesh.shape["val"]

    def program(trials, *rest):
        whole_lanes = trials.shape[2] % 128 == 0 and rest[0].shape[1] % 128 == 0
        if whole_lanes and trials.shape[0] == 2 and n_pts == 8 and n_val <= 4:
            return fused(n_pts, n_val, trials, *rest)
        return local(trials, *rest)

    in_specs = (
        P(None, "val", "pts"),
        P("pts", "val"),
        P("pts", None),
        P(None, ("pts", "val")),
        P("val"),
        P(),
    )
    out_specs = (P(None, "val", "pts"), P(None, "val", "pts"))
    return jax.shard_map(program, mesh=mesh, in_specs=in_specs, out_specs=out_specs, check_vma=False)
```

```python
import jax
import jax.numpy as jnp
from jax import lax
from jax.experimental import pallas as pl
from jax.experimental.pallas import tpu as pltpu
from jax.sharding import PartitionSpec as P

center_shift = 1.75
half_width = 1.25


def gathered_inner(local_trial, psi_cond):
    return jnp.einsum(
        "kvc,mc->kvm",
        lax.all_gather(local_trial, "pts", axis=2, tiled=True),
        psi_cond,
        preferred_element_type=jnp.float32,
    )


def orbital_terms(inner, psi_val, psi_cond, kernel):
    rho_part = jnp.einsum("mv,kvm->km", psi_val.astype(jnp.float32), inner)
    rho = lax.psum_scatter(rho_part, "val", scatter_dimension=1, tiled=True).astype(jnp.bfloat16)
    image_part = jnp.einsum("km,nm->kn", rho, kernel, preferred_element_type=jnp.float32)
    image_rows = lax.psum_scatter(
        image_part.astype(jnp.bfloat16), "pts", scatter_dimension=1, tiled=True
    ).astype(jnp.float32)
    image = lax.psum(image_rows, "val")
    weighted = (jnp.transpose(psi_val.astype(jnp.float32))[None] * image[:, None, :]).astype(
        jnp.bfloat16
    )
    return jnp.einsum("kvm,mc->kvc", weighted, psi_cond, preferred_element_type=jnp.float32)


def reduced(partial_sum):
    return lax.psum_scatter(
        partial_sum.astype(jnp.bfloat16), "pts", scatter_dimension=2, tiled=True
    ).astype(jnp.float32)


def local(trials, psi_val, psi_cond, kernel, eps_val, eps_cond):
    cols_own = trials.shape[2]
    index_pts = lax.axis_index("pts")
    diff_whole = (eps_cond[None, :] - eps_val[:, None] - center_shift)[None]
    diff_own = lax.dynamic_slice_in_dim(diff_whole, index_pts * cols_own, cols_own, 2)
    first_image = reduced(
        orbital_terms(gathered_inner(trials, psi_cond), psi_val, psi_cond, kernel)
    )
    first = (diff_own * trials.astype(jnp.float32) + 2.0 * first_image) / half_width
    second_trial = first.astype(jnp.bfloat16)
    second_inner = gathered_inner(second_trial, psi_cond)
    second_image = reduced(orbital_terms(second_inner, psi_val, psi_cond, kernel))
    filtered = 2.0 * (
        diff_own * second_trial.astype(jnp.float32) + 2.0 * second_image
    ) / half_width - trials.astype(jnp.float32)
    return (first, filtered)


F32, BF16 = jnp.float32, jnp.bfloat16
NT = (((1,), (1,)), ((), ()))


def fused_kernel(n_pts, n_val, x_hbm, pv_hbm, pc_hbm, kern_hbm, ev_hbm, ec_hbm, first_ref, filt_ref,
                 x_ref, pv, pvt, cond, kern, kern_t, ev_ref, ec_ref, diff, second, xg, rs, rr, im, ir,
                 acc, part_out, part_in, load_sem, mate_send, mate_recv, send_sem, recv_sem):
    p = lax.axis_index("pts")
    z = lax.axis_index("val")
    n_k, rows, cols = x_ref.shape
    pts_own = pv.shape[1]
    width = rr.shape[-1] // 2
    lanes = ir.shape[-1]
    step = 256

    def flipped(q, bit):
        return q + bit - 2 * bit * lax.rem(lax.div(q, bit), 2)

    mate = flipped(p, 1)
    core = lax.rem(p, 2)
    chips = (p, flipped(p, 2), flipped(p, 4), flipped(flipped(p, 2), 4))

    def served(core):
        x_turn, y_turn = flipped(p, 2) - p, flipped(p, 4) - p
        return lax.div(p + y_turn + (1 - core) * x_turn, 2), lax.div(p + core * x_turn, 2)

    load_x = pltpu.make_async_copy(x_hbm, x_ref, load_sem.at[0])
    load_x.start()
    barrier = pltpu.get_barrier_semaphore()
    for to in (*chips[1:], mate):
        pl.semaphore_signal(barrier, inc=1, device_id=(to, z), device_id_type=pl.DeviceIdType.MESH)
    for s in range(1, n_val):
        for to in (p, mate):
            pl.semaphore_signal(barrier, inc=1, device_id=(to, lax.rem(z + s, n_val)), device_id_type=pl.DeviceIdType.MESH)
    load_pv = pltpu.make_async_copy(pv_hbm, pv.at[0], load_sem.at[1])
    load_pv.start()
    for d in range(4):
        at = pl.multiple_of(chips[d] * cols, cols)
        pltpu.make_async_copy(
            pc_hbm.at[:, pl.ds(at, cols)], cond.at[0, d // 2, :, pl.ds(d % 2 * cols, cols)], load_sem.at[2]).start()
    load_ev = pltpu.make_async_copy(ev_hbm, ev_ref, load_sem.at[3])
    load_ec = pltpu.make_async_copy(ec_hbm, ec_ref, load_sem.at[4])
    load_ev.start()
    load_ec.start()
    load_x.wait()
    pl.semaphore_wait(barrier, 4 + 2 * (n_val - 1))

    groups = {
        "x_near": lambda it, k: xg.at[it, k, 0],
        "x_far": lambda it, k: xg.at[it, k, 1:3],
        "rho": lambda it, k: rr.at[it, k, 1:2 * n_val],
        "image": lambda it, k: ir.at[it, k],
        "pairs": lambda it, k: part_in.at[it, k],
    }
    places = {name: at for at, name in enumerate(groups)}

    def wait_for(ref, sem):
        pltpu.make_async_copy(ref, ref, sem).wait()

    def remote(it, k, group, src, dst, to_p, to_z):
        n = places[group]
        pltpu.make_async_remote_copy(
            src_ref=src, dst_ref=dst, send_sem=send_sem.at[it, k, n], recv_sem=recv_sem.at[it, k, n],
            device_id=(to_p, to_z), device_id_type=pl.DeviceIdType.MESH).start()

    def arrived(it, k, group):
        wait_for(groups[group](it, k), recv_sem.at[it, k, places[group]])

    def sent(it, k, group):
        if group == "image":
            image_wait(it, k, send_sem)
        else:
            wait_for(groups[group](it, k), send_sem.at[it, k, places[group]])

    def gather_start(it, k, x):
        for d in (3, 1, 2):
            remote(it, k, "x_near" if d == 1 else "x_far", x.at[k], xg.at[it, k, d - 1], chips[d], z)

    def to_mate(n, src, dst):
        pltpu.make_async_remote_copy(
            src_ref=src, dst_ref=dst, send_sem=mate_send.at[n], recv_sem=mate_recv.at[n],
            device_id=(mate, z), device_id_type=pl.DeviceIdType.MESH).start()

    def density(it, k, jj, left, right, rho):
        block = jnp.concatenate([left, right], axis=1)
        out = []
        for b in range(2):
            for t in range(pts_own // step):
                zz = lax.dot_general(block, cond[b, jj, t * step:(t + 1) * step, :], NT, preferred_element_type=F32)
                y = zz * pvt[b, :, t * step:(t + 1) * step]
                out.append(jnp.sum(y.reshape(rows // 8, 8, step), axis=0))
        return out if rho is None else [u + w for u, w in zip(rho, out)]

    def rho_start(it, k, rho):
        row = jnp.concatenate([jnp.sum(u, axis=0, keepdims=True) for u in rho], axis=1)
        for s in range(n_val):
            for b in range(2):
                tile = row[:, b * pts_own + s * width:b * pts_own + (s + 1) * width]
                rs[it, k, 0, s, :, b * width:(b + 1) * width] = tile
                rs[it, k, 1, s, :, (1 - b) * width:(2 - b) * width] = tile
        for s in range(n_val - 1, -1, -1):
            to = lax.rem(z + s, n_val)
            for b in range(2):
                if b or s:
                    remote(it, k, "rho", rs.at[it, k, b, to], rr.at[it, k, n_val * b + s], mate if b else p, to)

    def tiled(part):
        sub = lax.broadcasted_iota(jnp.int32, (8, lanes), 0)
        out = part[:, :lanes]
        for i in range(1, pts_own // lanes):
            out = jnp.where(sub == i, part[:, i * lanes:(i + 1) * lanes], out)
        return out

    def image_wait(it, k, sem):
        @pl.when(core == 0)
        def _():
            wait_for(ir.at[it, k, 1:], sem.at[it, k, places["image"]])

        @pl.when(core == 1)
        def _():
            wait_for(ir.at[it, k], sem.at[it, k, places["image"]])

    def image_start(it, k):
        own = rs[it, k, 0, z]
        arrived(it, k, "rho")
        for i in range(1, 2 * n_val):
            own = own + rr[it, k, i]
        own = jnp.broadcast_to(own, (8, 2 * width)).astype(BF16)
        for j in range(2):
            part = jnp.dot(own, kern_t[j], preferred_element_type=F32)
            part = jnp.concatenate([tiled(part[:, :pts_own]), tiled(part[:, pts_own:])], axis=0).astype(BF16)
            im[it, k, j] = part
            slot = (3 - core) if j == 0 else core
            for s in range(n_val - 1, -1, -1):
                to = lax.rem(z + s, n_val)

                def send(to_core):
                    remote(it, k, "image", im.at[it, k, j], ir.at[it, k, 4 * s + slot],
                           2 * served(core)[j] + to_core, to)

                if s or j == 0:
                    send(0)
                else:
                    @pl.when(core == 0)
                    def _():
                        ir[it, k, 0] = part

                    @pl.when(core == 1)
                    def _():
                        send(0)
                send(1)

    def pairs_start(it, k):
        image_wait(it, k, recv_sem)
        total = ir[it, k, 0].astype(F32)
        for i in range(1, 4 * n_val):
            total = total + ir[it, k, i].astype(F32)
        low, high = total[:8], total[8:]
        weighted = []
        for b in range(2):
            total = jnp.where(core == b, low, high)
            row = jnp.concatenate([total[i:i + 1] for i in range(pts_own // lanes)], axis=1)
            weighted.append((pvt[b] * row).astype(BF16))
        for jj in (1, 0):
            both = (jnp.dot(weighted[0], cond[0, jj], preferred_element_type=F32)
                    + jnp.dot(weighted[1], cond[1, jj], preferred_element_type=F32))
            for d in ((3, 2), (1, 0))[1 - jj]:
                tile = both[:, d % 2 * cols:(d % 2 + 1) * cols]
                if d == 0:
                    acc[k] = tile
                else:
                    part_out[it, k, d - 1] = tile.astype(BF16)
                    remote(it, k, "pairs", part_out.at[it, k, d - 1], part_in.at[it, k, d - 1], chips[d], z)

    def pairs_end(it, k):
        value = acc[k]
        arrived(it, k, "pairs")
        for d in (1, 2, 3):
            value = value + part_in[it, k, d - 1].astype(F32)
        return value

    def apply(it, x, use):
        every = range(n_k)
        if it == 0:
            for k in every:
                gather_start(it, k, x)
            to_mate(0, pv_hbm, pv.at[1])
            for d in range(4):
                at = pl.multiple_of(flipped(chips[d], 1) * cols, cols)
                to_mate(1, pc_hbm.at[:, pl.ds(at, cols)], cond.at[1, d // 2, :, pl.ds(d % 2 * cols, cols)])
            for j in range(2):
                part = pl.ds(pl.multiple_of(served(1 - core)[j] * 2 * pts_own, 2 * pts_own), 2 * pts_own)
                to_mate(2, kern_hbm.at[part], kern.at[1, j])
            for j in range(2):
                part = pl.ds(pl.multiple_of(served(core)[j] * 2 * pts_own, 2 * pts_own), 2 * pts_own)
                pltpu.make_async_copy(kern_hbm.at[part], kern.at[0, j], load_sem.at[5]).start()
            load_ev.wait()
            load_ec.wait()
            diff[...] = (ec_ref[:, pl.ds(pl.multiple_of(p * cols, cols), cols)]
                         - jnp.transpose(jnp.broadcast_to(ev_ref[...], (cols, rows))) - center_shift)
            load_pv.wait()
            pvt[0] = jnp.transpose(pv[0].astype(F32))
            wait_for(pv.at[1], mate_recv.at[0])
            pvt[1] = jnp.transpose(pv[1].astype(F32))
            wait_for(cond.at[0], load_sem.at[2])
            wait_for(cond.at[1], mate_recv.at[1])
        for k in every:
            arrived(it, k, "x_near")
            rho = density(it, k, 0, x[k], xg[it, k, 0], None)
            arrived(it, k, "x_far")
            rho = density(it, k, 1, xg[it, k, 1], xg[it, k, 2], rho)
            rho_start(it, k, rho)
        if it == 0:
            for b in range(2):
                wait_for(kern.at[b], mate_recv.at[2] if b else load_sem.at[5])
                for j in range(2):
                    kern_t[j, b * width:(b + 1) * width] = jnp.transpose(kern[b, j])
        for stage in (image_start, pairs_start):
            for k in every:
                stage(it, k)
        if it == 1:
            for i in range(2):
                for k in every:
                    for group in groups:
                        if i == 0 or group != "pairs":
                            sent(i, k, group)
            for n, ref in enumerate((pv.at[1], cond.at[1], kern.at[1])):
                wait_for(ref, mate_send.at[n])
        for k in every:
            use(k, pairs_end(it, k))

    def to_first(k, image):
        value = (diff[...] * x_ref[k].astype(F32) + 2.0 * image) / half_width
        second[k] = value.astype(BF16)
        gather_start(1, k, second)
        first_ref[k] = value

    def to_filtered(k, image):
        filt_ref[k] = 2.0 * (diff[...] * second[k].astype(F32) + 2.0 * image) / half_width - x_ref[k].astype(F32)

    apply(0, x_ref, to_first)
    apply(1, second, to_filtered)
    for k in range(n_k):
        sent(1, k, "pairs")


def hand_over(a, b, a_out, b_out, sem):
    copies = [pltpu.make_async_copy(a, a_out, sem.at[0]), pltpu.make_async_copy(b, b_out, sem.at[1])]
    for copy in copies:
        copy.start()
    for copy in copies:
        copy.wait()


def fused(n_pts, n_val, trials, psi_val, psi_cond, kernel, eps_val, eps_cond):
    n_k, rows, cols = trials.shape
    points = psi_val.shape[0]
    width = kernel.shape[1]
    vmem, hbm = pl.BlockSpec(memory_space=pltpu.VMEM), pl.BlockSpec(memory_space=pl.ANY)
    tile = (n_k, rows, cols)
    image = (2 * points // 128, 128)
    kept = pltpu.VMEM(tile, F32)
    results = pl.pallas_call(
        lambda *refs: fused_kernel(n_pts, n_val, *refs),
        out_shape=(kept, kept),
        in_specs=[hbm] * 6,
        out_specs=(vmem, vmem),
        scratch_shapes=[
            pltpu.VMEM(tile, BF16),
            pltpu.VMEM((2, points, rows), BF16),
            pltpu.VMEM((2, rows, points), F32),
            pltpu.VMEM((2, 2, points, 2 * cols), BF16),
            pltpu.VMEM((2, 2, 2 * points, width), BF16),
            pltpu.VMEM((2, 2 * width, 2 * points), BF16),
            pltpu.VMEM((1, rows), F32),
            pltpu.VMEM((1, eps_cond.shape[0]), F32),
            pltpu.VMEM((rows, cols), F32),
            pltpu.VMEM(tile, BF16),
            pltpu.VMEM((2, n_k, 3, rows, cols), BF16),
            pltpu.VMEM((2, n_k, 2, n_val, 1, 2 * width), F32),
            pltpu.VMEM((2, n_k, 2 * n_val, 1, 2 * width), F32),
            pltpu.VMEM((2, n_k, 2) + image, BF16),
            pltpu.VMEM((2, n_k, 4 * n_val) + image, BF16),
            pltpu.VMEM(tile, F32),
            pltpu.VMEM((2, n_k, 3, rows, cols), BF16),
            pltpu.VMEM((2, n_k, 3, rows, cols), BF16),
            pltpu.SemaphoreType.DMA((6,)),
            pltpu.SemaphoreType.DMA((3,)),
            pltpu.SemaphoreType.DMA((3,)),
            pltpu.SemaphoreType.DMA((2, n_k, 5)),
            pltpu.SemaphoreType.DMA((2, n_k, 5)),
        ],
        compiler_params=pltpu.CompilerParams(
            collective_id=0, has_side_effects=True, vmem_limit_bytes=56 * 1024 * 1024),
    )(trials, psi_val, psi_cond, kernel, eps_val.reshape(1, -1), eps_cond.reshape(1, -1))
    out = jax.ShapeDtypeStruct(tile, F32)
    return pl.pallas_call(
        hand_over,
        out_shape=(out, out),
        in_specs=[hbm, hbm],
        out_specs=(hbm, hbm),
        scratch_shapes=[pltpu.SemaphoreType.DMA((2,))],
        compiler_params=pltpu.CompilerParams(vmem_limit_bytes=1024 * 1024),
    )(*results)


def solution(mesh):
    n_pts, n_val = mesh.shape["pts"], mesh.shape["val"]

    def program(trials, *rest):
        whole_lanes = trials.shape[2] % 128 == 0 and rest[0].shape[1] % 128 == 0
        if whole_lanes and trials.shape[0] == 2 and n_pts == 8 and n_val <= 4:
            return fused(n_pts, n_val, trials, *rest)
        return local(trials, *rest)

    in_specs = (
        P(None, "val", "pts"),
        P("pts", "val"),
        P("pts", None),
        P(None, ("pts", "val")),
        P("val"),
        P(),
    )
    out_specs = (P(None, "val", "pts"), P(None, "val", "pts"))
    return jax.shard_map(program, mesh=mesh, in_specs=in_specs, out_specs=out_specs, check_vma=False)
```

```python
import jax
import jax.numpy as jnp
from jax import lax
from jax.experimental import pallas as pl
from jax.experimental.pallas import tpu as pltpu
from jax.sharding import PartitionSpec as P

center_shift = 1.75
half_width = 1.25


def gathered_inner(local_trial, psi_cond):
    return jnp.einsum(
        "kvc,mc->kvm",
        lax.all_gather(local_trial, "pts", axis=2, tiled=True),
        psi_cond,
        preferred_element_type=jnp.float32,
    )


def orbital_terms(inner, psi_val, psi_cond, kernel):
    rho_part = jnp.einsum("mv,kvm->km", psi_val.astype(jnp.float32), inner)
    rho = lax.psum_scatter(rho_part, "val", scatter_dimension=1, tiled=True).astype(jnp.bfloat16)
    image_part = jnp.einsum("km,nm->kn", rho, kernel, preferred_element_type=jnp.float32)
    image_rows = lax.psum_scatter(
        image_part.astype(jnp.bfloat16), "pts", scatter_dimension=1, tiled=True
    ).astype(jnp.float32)
    image = lax.psum(image_rows, "val")
    weighted = (jnp.transpose(psi_val.astype(jnp.float32))[None] * image[:, None, :]).astype(
        jnp.bfloat16
    )
    return jnp.einsum("kvm,mc->kvc", weighted, psi_cond, preferred_element_type=jnp.float32)


def reduced(partial_sum):
    return lax.psum_scatter(
        partial_sum.astype(jnp.bfloat16), "pts", scatter_dimension=2, tiled=True
    ).astype(jnp.float32)


def local(trials, psi_val, psi_cond, kernel, eps_val, eps_cond):
    cols_own = trials.shape[2]
    index_pts = lax.axis_index("pts")
    diff_whole = (eps_cond[None, :] - eps_val[:, None] - center_shift)[None]
    diff_own = lax.dynamic_slice_in_dim(diff_whole, index_pts * cols_own, cols_own, 2)
    first_image = reduced(
        orbital_terms(gathered_inner(trials, psi_cond), psi_val, psi_cond, kernel)
    )
    first = (diff_own * trials.astype(jnp.float32) + 2.0 * first_image) / half_width
    second_trial = first.astype(jnp.bfloat16)
    second_inner = gathered_inner(second_trial, psi_cond)
    second_image = reduced(orbital_terms(second_inner, psi_val, psi_cond, kernel))
    filtered = 2.0 * (
        diff_own * second_trial.astype(jnp.float32) + 2.0 * second_image
    ) / half_width - trials.astype(jnp.float32)
    return (first, filtered)


F32, BF16 = jnp.float32, jnp.bfloat16
NT = (((1,), (1,)), ((), ()))


def fused_kernel(n_pts, n_val, x_hbm, pv_hbm, pc_hbm, kern_hbm, ev_hbm, ec_hbm, first_ref, filt_ref,
                 x_ref, pv, pvt, cond, kern, kern_t, ev_ref, ec_ref, diff, second, xg, rs, rr, im, ir,
                 acc, part_out, part_in, load_sem, mate_send, mate_recv, send_sem, recv_sem):
    p = lax.axis_index("pts")
    z = lax.axis_index("val")
    n_k, rows, cols = x_ref.shape
    pts_own = pv.shape[1]
    width = rr.shape[-1] // 2
    lanes = ir.shape[-1]
    step = 256

    def flipped(q, bit):
        return q + bit - 2 * bit * lax.rem(lax.div(q, bit), 2)

    mate = flipped(p, 1)
    core = lax.rem(p, 2)
    chips = (p, flipped(p, 2), flipped(p, 4), flipped(flipped(p, 2), 4))

    def served(core):
        x_turn, y_turn = flipped(p, 2) - p, flipped(p, 4) - p
        return lax.div(p + y_turn + (1 - core) * x_turn, 2), lax.div(p + core * x_turn, 2)

    load_x = pltpu.make_async_copy(x_hbm, x_ref, load_sem.at[0])
    load_x.start()
    barrier = pltpu.get_barrier_semaphore()
    for to in (*chips[1:], mate):
        pl.semaphore_signal(barrier, inc=1, device_id=(to, z), device_id_type=pl.DeviceIdType.MESH)
    for s in range(1, n_val):
        for to in (p, mate):
            pl.semaphore_signal(barrier, inc=1, device_id=(to, lax.rem(z + s, n_val)), device_id_type=pl.DeviceIdType.MESH)
    load_pv = pltpu.make_async_copy(pv_hbm, pv.at[0], load_sem.at[1])
    load_pv.start()
    for d in range(4):
        at = pl.multiple_of(chips[d] * cols, cols)
        pltpu.make_async_copy(
            pc_hbm.at[:, pl.ds(at, cols)], cond.at[0, d // 2, :, pl.ds(d % 2 * cols, cols)], load_sem.at[2]).start()
    load_ev = pltpu.make_async_copy(ev_hbm, ev_ref, load_sem.at[3])
    load_ec = pltpu.make_async_copy(ec_hbm, ec_ref, load_sem.at[4])
    load_ev.start()
    load_ec.start()
    load_x.wait()
    pl.semaphore_wait(barrier, 4 + 2 * (n_val - 1))

    groups = {
        "x_near": lambda it, k: xg.at[it, k, 0],
        "x_far": lambda it, k: xg.at[it, k, 1:3],
        "rho": lambda it, k: rr.at[it, k, 1:2 * n_val],
        "image": lambda it, k: ir.at[it, k],
        "pairs_top": lambda it, k: part_in.at[it, k, 0],
        "pairs_low": lambda it, k: part_in.at[it, k, 1],
    }
    places = {name: at for at, name in enumerate(groups)}

    def wait_for(ref, sem):
        pltpu.make_async_copy(ref, ref, sem).wait()

    def remote(it, k, group, src, dst, to_p, to_z):
        n = places[group]
        pltpu.make_async_remote_copy(
            src_ref=src, dst_ref=dst, send_sem=send_sem.at[n], recv_sem=recv_sem.at[k, n],
            device_id=(to_p, to_z), device_id_type=pl.DeviceIdType.MESH).start()

    def arrived(it, k, group):
        wait_for(groups[group](it, k), recv_sem.at[k, places[group]])

    halves = (("pairs_top", slice(0, rows // 2)), ("pairs_low", slice(rows // 2, rows)))

    def gather_start(it, k, half, x):
        part = halves[half][1]
        for d in (3, 1, 2):
            remote(it, k, "x_near" if d == 1 else "x_far", x.at[k, part], xg.at[it, k, d - 1, part], chips[d], z)

    def to_mate(n, src, dst):
        pltpu.make_async_remote_copy(
            src_ref=src, dst_ref=dst, send_sem=mate_send.at[n], recv_sem=mate_recv.at[n],
            device_id=(mate, z), device_id_type=pl.DeviceIdType.MESH).start()

    def density(it, k, jj, left, right, rho):
        block = jnp.concatenate([left, right], axis=1)
        out = []
        for b in range(2):
            for t in range(pts_own // step):
                zz = lax.dot_general(block, cond[b, jj, t * step:(t + 1) * step, :], NT, preferred_element_type=F32)
                y = zz * pvt[b, :, t * step:(t + 1) * step]
                out.append(jnp.sum(y.reshape(rows // 8, 8, step), axis=0))
        return out if rho is None else [u + w for u, w in zip(rho, out)]

    def rho_start(it, k, rho):
        row = jnp.concatenate([jnp.sum(u, axis=0, keepdims=True) for u in rho], axis=1)
        for s in range(n_val):
            for b in range(2):
                tile = row[:, b * pts_own + s * width:b * pts_own + (s + 1) * width]
                rs[it, k, 0, s, :, b * width:(b + 1) * width] = tile
                rs[it, k, 1, s, :, (1 - b) * width:(2 - b) * width] = tile
        for s in range(n_val - 1, -1, -1):
            to = lax.rem(z + s, n_val)
            for b in range(2):
                if b or s:
                    remote(it, k, "rho", rs.at[it, k, b, to], rr.at[it, k, n_val * b + s], mate if b else p, to)

    def tiled(part):
        sub = lax.broadcasted_iota(jnp.int32, (8, lanes), 0)
        out = part[:, :lanes]
        for i in range(1, pts_own // lanes):
            out = jnp.where(sub == i, part[:, i * lanes:(i + 1) * lanes], out)
        return out

    def image_wait(ref, sem):
        @pl.when(core == 0)
        def _():
            wait_for(ref.at[..., 1:, :, :], sem)

        @pl.when(core == 1)
        def _():
            wait_for(ref, sem)

    def image_start(it, k):
        own = rs[it, k, 0, z]
        arrived(it, k, "rho")
        for i in range(1, 2 * n_val):
            own = own + rr[it, k, i]
        own = jnp.broadcast_to(own, (8, 2 * width)).astype(BF16)
        for j in range(2):
            part = jnp.dot(own, kern_t[j], preferred_element_type=F32)
            part = jnp.concatenate([tiled(part[:, :pts_own]), tiled(part[:, pts_own:])], axis=0).astype(BF16)
            im[it, k, j] = part
            slot = (3 - core) if j == 0 else core
            for s in range(n_val - 1, -1, -1):
                to = lax.rem(z + s, n_val)

                def send(to_core):
                    remote(it, k, "image", im.at[it, k, j], ir.at[it, k, 4 * s + slot],
                           2 * served(core)[j] + to_core, to)

                if s or j == 0:
                    send(0)
                else:
                    @pl.when(core == 0)
                    def _():
                        ir[it, k, 0] = part

                    @pl.when(core == 1)
                    def _():
                        send(0)
                send(1)

    def pairs_start(it, k):
        image_wait(ir.at[it, k], recv_sem.at[k, places["image"]])
        total = ir[it, k, 0].astype(F32)
        for i in range(1, 4 * n_val):
            total = total + ir[it, k, i].astype(F32)
        low, high = total[:8], total[8:]
        images = []
        for b in range(2):
            total = jnp.where(core == b, low, high)
            row = jnp.concatenate([total[i:i + 1] for i in range(pts_own // lanes)], axis=1)
            images.append(row)
        left = [(pvt[b] * images[b]).astype(BF16) for b in range(2)]
        tiles = {}
        for jj in (1, 0):
            both = (jnp.dot(left[0], cond[0, jj], preferred_element_type=F32)
                    + jnp.dot(left[1], cond[1, jj], preferred_element_type=F32))
            for d in ((3, 2), (1, 0))[1 - jj]:
                tile = both[:, d % 2 * cols:(d % 2 + 1) * cols]
                if d == 0:
                    acc[k] = tile
                else:
                    for half, (group, part) in enumerate(halves):
                        part_out[it, k, half, d - 1] = tile[part].astype(BF16)
            if jj == 1:
                for half, (group, part) in enumerate(halves):
                    for d in (3, 2):
                        remote(it, k, group, part_out.at[it, k, half, d - 1], part_in.at[it, k, half, d - 1], chips[d], z)
        for half, (group, part) in enumerate(halves):
            for d in (1,):
                remote(it, k, group, part_out.at[it, k, half, d - 1], part_in.at[it, k, half, d - 1], chips[d], z)

    def pairs_end(it, k, half):
        group, part = halves[half]
        value = acc[k, part]
        arrived(it, k, group)
        for d in (1, 2, 3):
            value = value + part_in[it, k, half, d - 1].astype(F32)
        return value

    def apply(it, x, use):
        every = range(n_k)
        if it == 0:
            for k in every:
                for half in range(2):
                    gather_start(it, k, half, x)
            to_mate(0, pv_hbm, pv.at[1])
            for d in range(4):
                at = pl.multiple_of(flipped(chips[d], 1) * cols, cols)
                to_mate(1, pc_hbm.at[:, pl.ds(at, cols)], cond.at[1, d // 2, :, pl.ds(d % 2 * cols, cols)])
            for j in range(2):
                part = pl.ds(pl.multiple_of(served(1 - core)[j] * 2 * pts_own, 2 * pts_own), 2 * pts_own)
                to_mate(2, kern_hbm.at[part], kern.at[1, j])
            for j in range(2):
                part = pl.ds(pl.multiple_of(served(core)[j] * 2 * pts_own, 2 * pts_own), 2 * pts_own)
                pltpu.make_async_copy(kern_hbm.at[part], kern.at[0, j], load_sem.at[5]).start()
            load_ev.wait()
            load_ec.wait()
            diff[...] = (ec_ref[:, pl.ds(pl.multiple_of(p * cols, cols), cols)]
                         - jnp.transpose(jnp.broadcast_to(ev_ref[...], (cols, rows))) - center_shift)
            load_pv.wait()
            pvt[0] = jnp.transpose(pv[0].astype(F32))
            wait_for(pv.at[1], mate_recv.at[0])
            pvt[1] = jnp.transpose(pv[1].astype(F32))
            wait_for(cond.at[0], load_sem.at[2])
            wait_for(cond.at[1], mate_recv.at[1])
        for k in every:
            arrived(it, k, "x_near")
            rho = density(it, k, 0, x[k], xg[it, k, 0], None)
            arrived(it, k, "x_far")
            rho = density(it, k, 1, xg[it, k, 1], xg[it, k, 2], rho)
            rho_start(it, k, rho)
        if it == 0:
            for b in range(2):
                wait_for(kern.at[b], mate_recv.at[2] if b else load_sem.at[5])
                for j in range(2):
                    kern_t[j, b * width:(b + 1) * width] = jnp.transpose(kern[b, j])
        for stage in (image_start, pairs_start):
            for k in every:
                stage(it, k)
        if it == 1:
            for n, ref in enumerate((pv.at[1], cond.at[1], kern.at[1])):
                wait_for(ref, mate_send.at[n])
            wait_for(xg.at[:, :, 0], send_sem.at[places["x_near"]])
            wait_for(xg.at[:, :, 1:], send_sem.at[places["x_far"]])
            wait_for(rr.at[:, :, 1:], send_sem.at[places["rho"]])
            image_wait(ir, send_sem.at[places["image"]])
        for k in every:
            for half in range(2):
                use(k, half, pairs_end(it, k, half))

    def to_first(k, half, image):
        part = halves[half][1]
        value = (diff[part] * x_ref[k, part].astype(F32) + 2.0 * image) / half_width
        second[k, part] = value.astype(BF16)
        gather_start(1, k, half, second)
        first_ref[k, part] = value

    def to_filtered(k, half, image):
        part = halves[half][1]
        filt_ref[k, part] = (2.0 * (diff[part] * second[k, part].astype(F32) + 2.0 * image) / half_width
                             - x_ref[k, part].astype(F32))

    apply(0, x_ref, to_first)
    apply(1, second, to_filtered)
    for half, (group, part) in enumerate(halves):
        wait_for(part_in.at[:, :, half], send_sem.at[places[group]])


def hand_over(a, b, a_out, b_out, sem):
    copies = [pltpu.make_async_copy(a, a_out, sem.at[0]), pltpu.make_async_copy(b, b_out, sem.at[1])]
    for copy in copies:
        copy.start()
    for copy in copies:
        copy.wait()


def fused(n_pts, n_val, trials, psi_val, psi_cond, kernel, eps_val, eps_cond):
    n_k, rows, cols = trials.shape
    points = psi_val.shape[0]
    width = kernel.shape[1]
    vmem, hbm = pl.BlockSpec(memory_space=pltpu.VMEM), pl.BlockSpec(memory_space=pl.ANY)
    tile = (n_k, rows, cols)
    image = (2 * points // 128, 128)
    kept = pltpu.VMEM(tile, F32)
    results = pl.pallas_call(
        lambda *refs: fused_kernel(n_pts, n_val, *refs),
        out_shape=(kept, kept),
        in_specs=[hbm] * 6,
        out_specs=(vmem, vmem),
        scratch_shapes=[
            pltpu.VMEM(tile, BF16),
            pltpu.VMEM((2, points, rows), BF16),
            pltpu.VMEM((2, rows, points), F32),
            pltpu.VMEM((2, 2, points, 2 * cols), BF16),
            pltpu.VMEM((2, 2, 2 * points, width), BF16),
            pltpu.VMEM((2, 2 * width, 2 * points), BF16),
            pltpu.VMEM((1, rows), F32),
            pltpu.VMEM((1, eps_cond.shape[0]), F32),
            pltpu.VMEM((rows, cols), F32),
            pltpu.VMEM(tile, BF16),
            pltpu.VMEM((2, n_k, 3, rows, cols), BF16),
            pltpu.VMEM((2, n_k, 2, n_val, 1, 2 * width), F32),
            pltpu.VMEM((2, n_k, 2 * n_val, 1, 2 * width), F32),
            pltpu.VMEM((2, n_k, 2) + image, BF16),
            pltpu.VMEM((2, n_k, 4 * n_val) + image, BF16),
            pltpu.VMEM(tile, F32),
            pltpu.VMEM((2, n_k, 2, 3, rows // 2, cols), BF16),
            pltpu.VMEM((2, n_k, 2, 3, rows // 2, cols), BF16),
            pltpu.SemaphoreType.DMA((6,)),
            pltpu.SemaphoreType.DMA((3,)),
            pltpu.SemaphoreType.DMA((3,)),
            pltpu.SemaphoreType.DMA((6,)),
            pltpu.SemaphoreType.DMA((n_k, 6)),
        ],
        compiler_params=pltpu.CompilerParams(
            collective_id=0, has_side_effects=True, vmem_limit_bytes=56 * 1024 * 1024),
    )(trials, psi_val, psi_cond, kernel, eps_val.reshape(1, -1), eps_cond.reshape(1, -1))
    out = jax.ShapeDtypeStruct(tile, F32)
    return pl.pallas_call(
        hand_over,
        out_shape=(out, out),
        in_specs=[hbm, hbm],
        out_specs=(hbm, hbm),
        scratch_shapes=[pltpu.SemaphoreType.DMA((2,))],
        compiler_params=pltpu.CompilerParams(vmem_limit_bytes=1024 * 1024),
    )(*results)


def solution(mesh):
    n_pts, n_val = mesh.shape["pts"], mesh.shape["val"]

    def program(trials, *rest):
        whole_lanes = trials.shape[2] % 128 == 0 and rest[0].shape[1] % 128 == 0
        if whole_lanes and trials.shape[0] == 2 and n_pts == 8 and n_val <= 4:
            return fused(n_pts, n_val, trials, *rest)
        return local(trials, *rest)

    in_specs = (
        P(None, "val", "pts"),
        P("pts", "val"),
        P("pts", None),
        P(None, ("pts", "val")),
        P("val"),
        P(),
    )
    out_specs = (P(None, "val", "pts"), P(None, "val", "pts"))
    return jax.shard_map(program, mesh=mesh, in_specs=in_specs, out_specs=out_specs, check_vma=False)
```

```python
import jax
import jax.numpy as jnp
from jax import lax
from jax.experimental import pallas as pl
from jax.experimental.pallas import tpu as pltpu
from jax.sharding import PartitionSpec as P

center_shift = 1.75
half_width = 1.25


def gathered_inner(local_trial, psi_cond):
    return jnp.einsum(
        "kvc,mc->kvm",
        lax.all_gather(local_trial, "pts", axis=2, tiled=True),
        psi_cond,
        preferred_element_type=jnp.float32,
    )


def orbital_terms(inner, psi_val, psi_cond, kernel):
    rho_part = jnp.einsum("mv,kvm->km", psi_val.astype(jnp.float32), inner)
    rho = lax.psum_scatter(rho_part, "val", scatter_dimension=1, tiled=True).astype(jnp.bfloat16)
    image_part = jnp.einsum("km,nm->kn", rho, kernel, preferred_element_type=jnp.float32)
    image_rows = lax.psum_scatter(
        image_part.astype(jnp.bfloat16), "pts", scatter_dimension=1, tiled=True
    ).astype(jnp.float32)
    image = lax.psum(image_rows, "val")
    weighted = (jnp.transpose(psi_val.astype(jnp.float32))[None] * image[:, None, :]).astype(
        jnp.bfloat16
    )
    return jnp.einsum("kvm,mc->kvc", weighted, psi_cond, preferred_element_type=jnp.float32)


def reduced(partial_sum):
    return lax.psum_scatter(
        partial_sum.astype(jnp.bfloat16), "pts", scatter_dimension=2, tiled=True
    ).astype(jnp.float32)


def local(trials, psi_val, psi_cond, kernel, eps_val, eps_cond):
    cols_own = trials.shape[2]
    index_pts = lax.axis_index("pts")
    diff_whole = (eps_cond[None, :] - eps_val[:, None] - center_shift)[None]
    diff_own = lax.dynamic_slice_in_dim(diff_whole, index_pts * cols_own, cols_own, 2)
    first_image = reduced(
        orbital_terms(gathered_inner(trials, psi_cond), psi_val, psi_cond, kernel)
    )
    first = (diff_own * trials.astype(jnp.float32) + 2.0 * first_image) / half_width
    second_trial = first.astype(jnp.bfloat16)
    second_inner = gathered_inner(second_trial, psi_cond)
    second_image = reduced(orbital_terms(second_inner, psi_val, psi_cond, kernel))
    filtered = 2.0 * (
        diff_own * second_trial.astype(jnp.float32) + 2.0 * second_image
    ) / half_width - trials.astype(jnp.float32)
    return (first, filtered)


F32, BF16 = jnp.float32, jnp.bfloat16
NT = (((1,), (1,)), ((), ()))


def fused_kernel(n_pts, n_val, x_hbm, pv_hbm, pc_hbm, kern_hbm, ev_hbm, ec_hbm, first_ref, filt_ref,
                 x_ref, pv, pvt, cond, kern, kern_t, ev_ref, ec_ref, diff, second, xg, rs, rr, im, ir,
                 acc, part_out, part_in, load_sem, mate_send, mate_recv, send_sem, recv_sem, met_sem):
    p = lax.axis_index("pts")
    z = lax.axis_index("val")
    n_k, rows, cols = x_ref.shape
    pts_own = pv.shape[1]
    width = rr.shape[-1] // 2
    lanes = ir.shape[-1]
    step = 256

    def flipped(q, bit):
        return q + bit - 2 * bit * lax.rem(lax.div(q, bit), 2)

    mate = flipped(p, 1)
    core = lax.rem(p, 2)
    chips = (p, flipped(p, 2), flipped(p, 4), flipped(flipped(p, 2), 4))

    def served(core):
        x_turn, y_turn = flipped(p, 2) - p, flipped(p, 4) - p
        return lax.div(p + y_turn + (1 - core) * x_turn, 2), lax.div(p + core * x_turn, 2)

    load_x = pltpu.make_async_copy(x_hbm, x_ref, load_sem.at[0])
    load_x.start()
    barrier = pltpu.get_barrier_semaphore()
    for to in (*chips[1:], mate):
        pl.semaphore_signal(barrier, inc=1, device_id=(to, z), device_id_type=pl.DeviceIdType.MESH)
    below = lax.div(z + n_val - 1, n_val)
    above = lax.div(2 * n_val - 2 - z, n_val)
    sides = ((below, z - below), (above, z + above))
    for there, at in sides:
        @pl.when(there == 1)
        def _():
            for to in (p, mate):
                pl.semaphore_signal(barrier, inc=1, device_id=(to, at), device_id_type=pl.DeviceIdType.MESH)
    load_pv = pltpu.make_async_copy(pv_hbm, pv.at[0], load_sem.at[1])
    load_pv.start()
    for d in range(4):
        at = pl.multiple_of(chips[d] * cols, cols)
        pltpu.make_async_copy(
            pc_hbm.at[:, pl.ds(at, cols)], cond.at[0, d // 2, :, pl.ds(d % 2 * cols, cols)], load_sem.at[2]).start()
    load_ev = pltpu.make_async_copy(ev_hbm, ev_ref, load_sem.at[3])
    load_ec = pltpu.make_async_copy(ec_hbm, ec_ref, load_sem.at[4])
    load_ev.start()
    load_ec.start()
    load_x.wait()
    pl.semaphore_wait(barrier, 4 + 2 * (below + above))

    def tell(turn):
        for side, (there, at) in enumerate(sides):
            @pl.when(there == 1)
            def _():
                pl.semaphore_signal(met_sem.at[turn, 1 - side], inc=1, device_id=(p, at),
                                    device_id_type=pl.DeviceIdType.MESH)

    def told(turn):
        for side, (there, at) in enumerate(sides):
            @pl.when(there == 1)
            def _():
                pl.semaphore_wait(met_sem.at[turn, side], 1)

    groups = {
        "x_near": lambda it, k: xg.at[it, k, 0],
        "x_far": lambda it, k: xg.at[it, k, 1:3],
        "rho": lambda it, k: rr.at[it, k, 1:2 * n_val],
        "image": lambda it, k: ir.at[it, k],
        "pairs_top": lambda it, k: part_in.at[it, k, 0],
        "pairs_low": lambda it, k: part_in.at[it, k, 1],
    }
    places = {name: at for at, name in enumerate(groups)}

    def wait_for(ref, sem):
        pltpu.make_async_copy(ref, ref, sem).wait()

    def remote(it, k, group, src, dst, to_p, to_z):
        n = places[group]
        pltpu.make_async_remote_copy(
            src_ref=src, dst_ref=dst, send_sem=send_sem.at[n], recv_sem=recv_sem.at[k, n],
            device_id=(to_p, to_z), device_id_type=pl.DeviceIdType.MESH).start()

    def arrived(it, k, group):
        wait_for(groups[group](it, k), recv_sem.at[k, places[group]])

    halves = (("pairs_top", slice(0, rows // 2)), ("pairs_low", slice(rows // 2, rows)))

    def gather_start(it, k, half, x):
        part = halves[half][1]
        for d in (3, 1, 2):
            remote(it, k, "x_near" if d == 1 else "x_far", x.at[k, part], xg.at[it, k, d - 1, part], chips[d], z)

    def to_mate(n, src, dst):
        pltpu.make_async_remote_copy(
            src_ref=src, dst_ref=dst, send_sem=mate_send.at[n], recv_sem=mate_recv.at[n],
            device_id=(mate, z), device_id_type=pl.DeviceIdType.MESH).start()

    def density(it, k, jj, left, right, rho):
        block = jnp.concatenate([left, right], axis=1)
        out = []
        for b in range(2):
            for t in range(pts_own // step):
                zz = lax.dot_general(block, cond[b, jj, t * step:(t + 1) * step, :], NT, preferred_element_type=F32)
                y = zz * pvt[b, :, t * step:(t + 1) * step]
                out.append(jnp.sum(y.reshape(rows // 8, 8, step), axis=0))
        return out if rho is None else [u + w for u, w in zip(rho, out)]

    def rho_start(it, k, rho):
        row = jnp.concatenate([jnp.sum(u, axis=0, keepdims=True) for u in rho], axis=1)
        for s in range(n_val):
            for b in range(2):
                tile = row[:, b * pts_own + s * width:b * pts_own + (s + 1) * width]
                rs[it, k, 0, s, :, b * width:(b + 1) * width] = tile
                rs[it, k, 1, s, :, (1 - b) * width:(2 - b) * width] = tile
        for s in range(n_val - 1, -1, -1):
            to = lax.rem(z + s, n_val)
            for b in range(2):
                if b or s:
                    remote(it, k, "rho", rs.at[it, k, b, to], rr.at[it, k, n_val * b + s], mate if b else p, to)

    def tiled(part):
        sub = lax.broadcasted_iota(jnp.int32, (8, lanes), 0)
        out = part[:, :lanes]
        for i in range(1, pts_own // lanes):
            out = jnp.where(sub == i, part[:, i * lanes:(i + 1) * lanes], out)
        return out

    def image_wait(ref, sem):
        @pl.when(core == 0)
        def _():
            wait_for(ref.at[..., 1:, :, :], sem)

        @pl.when(core == 1)
        def _():
            wait_for(ref, sem)

    def image_start(it, k):
        own = rs[it, k, 0, z]
        arrived(it, k, "rho")
        for i in range(1, 2 * n_val):
            own = own + rr[it, k, i]
        own = jnp.broadcast_to(own, (8, 2 * width)).astype(BF16)
        for j in range(2):
            part = jnp.dot(own, kern_t[j], preferred_element_type=F32)
            part = jnp.concatenate([tiled(part[:, :pts_own]), tiled(part[:, pts_own:])], axis=0).astype(BF16)
            im[it, k, j] = part
            slot = (3 - core) if j == 0 else core
            for s in range(n_val - 1, -1, -1):
                to = lax.rem(z + s, n_val)

                def send(to_core):
                    remote(it, k, "image", im.at[it, k, j], ir.at[it, k, 4 * s + slot],
                           2 * served(core)[j] + to_core, to)

                if s or j == 0:
                    send(0)
                else:
                    @pl.when(core == 0)
                    def _():
                        ir[it, k, 0] = part

                    @pl.when(core == 1)
                    def _():
                        send(0)
                send(1)

    def pairs_start(it, k):
        image_wait(ir.at[it, k], recv_sem.at[k, places["image"]])
        total = ir[it, k, 0].astype(F32)
        for i in range(1, 4 * n_val):
            total = total + ir[it, k, i].astype(F32)
        low, high = total[:8], total[8:]
        images = []
        for b in range(2):
            total = jnp.where(core == b, low, high)
            row = jnp.concatenate([total[i:i + 1] for i in range(pts_own // lanes)], axis=1)
            images.append(row)
        left = [(pvt[b] * images[b]).astype(BF16) for b in range(2)]
        tiles = {}
        for jj in (1, 0):
            both = (jnp.dot(left[0], cond[0, jj], preferred_element_type=F32)
                    + jnp.dot(left[1], cond[1, jj], preferred_element_type=F32))
            for d in ((3, 2), (1, 0))[1 - jj]:
                tile = both[:, d % 2 * cols:(d % 2 + 1) * cols]
                if d == 0:
                    acc[k] = tile
                else:
                    for half, (group, part) in enumerate(halves):
                        part_out[it, k, half, d - 1] = tile[part].astype(BF16)
            if jj == 1:
                for half, (group, part) in enumerate(halves):
                    for d in (3, 2):
                        remote(it, k, group, part_out.at[it, k, half, d - 1], part_in.at[it, k, half, d - 1], chips[d], z)
        for half, (group, part) in enumerate(halves):
            for d in (1,):
                remote(it, k, group, part_out.at[it, k, half, d - 1], part_in.at[it, k, half, d - 1], chips[d], z)

    def pairs_end(it, k, half):
        group, part = halves[half]
        value = acc[k, part]
        arrived(it, k, group)
        for d in (1, 2, 3):
            value = value + part_in[it, k, half, d - 1].astype(F32)
        return value

    def apply(it, x, use):
        every = range(n_k)
        if it == 0:
            for k in every:
                for half in range(2):
                    gather_start(it, k, half, x)
            tell(0)
            to_mate(0, pv_hbm, pv.at[1])
            for d in range(4):
                at = pl.multiple_of(flipped(chips[d], 1) * cols, cols)
                to_mate(1, pc_hbm.at[:, pl.ds(at, cols)], cond.at[1, d // 2, :, pl.ds(d % 2 * cols, cols)])
            for j in range(2):
                part = pl.ds(pl.multiple_of(served(1 - core)[j] * 2 * pts_own, 2 * pts_own), 2 * pts_own)
                to_mate(2, kern_hbm.at[part], kern.at[1, j])
            for j in range(2):
                part = pl.ds(pl.multiple_of(served(core)[j] * 2 * pts_own, 2 * pts_own), 2 * pts_own)
                pltpu.make_async_copy(kern_hbm.at[part], kern.at[0, j], load_sem.at[5]).start()
            load_ev.wait()
            load_ec.wait()
            diff[...] = (ec_ref[:, pl.ds(pl.multiple_of(p * cols, cols), cols)]
                         - jnp.transpose(jnp.broadcast_to(ev_ref[...], (cols, rows))) - center_shift)
            load_pv.wait()
            pvt[0] = jnp.transpose(pv[0].astype(F32))
            told(0)
            tell(1)
            wait_for(pv.at[1], mate_recv.at[0])
            pvt[1] = jnp.transpose(pv[1].astype(F32))
            wait_for(cond.at[0], load_sem.at[2])
            wait_for(cond.at[1], mate_recv.at[1])
        for k in every:
            arrived(it, k, "x_near")
            rho = density(it, k, 0, x[k], xg[it, k, 0], None)
            arrived(it, k, "x_far")
            rho = density(it, k, 1, xg[it, k, 1], xg[it, k, 2], rho)
            if it == 0 and k == 0:
                told(1)
            rho_start(it, k, rho)
        if it == 0:
            for b in range(2):
                wait_for(kern.at[b], mate_recv.at[2] if b else load_sem.at[5])
                for j in range(2):
                    kern_t[j, b * width:(b + 1) * width] = jnp.transpose(kern[b, j])
        for stage in (image_start, pairs_start):
            for k in every:
                stage(it, k)
        if it == 1:
            for n, ref in enumerate((pv.at[1], cond.at[1], kern.at[1])):
                wait_for(ref, mate_send.at[n])
            wait_for(xg.at[:, :, 0], send_sem.at[places["x_near"]])
            wait_for(xg.at[:, :, 1:], send_sem.at[places["x_far"]])
            wait_for(rr.at[:, :, 1:], send_sem.at[places["rho"]])
            image_wait(ir, send_sem.at[places["image"]])
        for k in every:
            for half in range(2):
                use(k, half, pairs_end(it, k, half))

    def to_first(k, half, image):
        part = halves[half][1]
        value = (diff[part] * x_ref[k, part].astype(F32) + 2.0 * image) / half_width
        second[k, part] = value.astype(BF16)
        gather_start(1, k, half, second)
        first_ref[k, part] = value

    def to_filtered(k, half, image):
        part = halves[half][1]
        filt_ref[k, part] = (2.0 * (diff[part] * second[k, part].astype(F32) + 2.0 * image) / half_width
                             - x_ref[k, part].astype(F32))

    apply(0, x_ref, to_first)
    apply(1, second, to_filtered)
    for half, (group, part) in enumerate(halves):
        wait_for(part_in.at[:, :, half], send_sem.at[places[group]])


def hand_over(a, b, a_out, b_out, sem):
    copies = [pltpu.make_async_copy(a, a_out, sem.at[0]), pltpu.make_async_copy(b, b_out, sem.at[1])]
    for copy in copies:
        copy.start()
    for copy in copies:
        copy.wait()


def fused(n_pts, n_val, trials, psi_val, psi_cond, kernel, eps_val, eps_cond):
    n_k, rows, cols = trials.shape
    points = psi_val.shape[0]
    width = kernel.shape[1]
    vmem, hbm = pl.BlockSpec(memory_space=pltpu.VMEM), pl.BlockSpec(memory_space=pl.ANY)
    tile = (n_k, rows, cols)
    image = (2 * points // 128, 128)
    kept = pltpu.VMEM(tile, F32)
    results = pl.pallas_call(
        lambda *refs: fused_kernel(n_pts, n_val, *refs),
        out_shape=(kept, kept),
        in_specs=[hbm] * 6,
        out_specs=(vmem, vmem),
        scratch_shapes=[
            pltpu.VMEM(tile, BF16),
            pltpu.VMEM((2, points, rows), BF16),
            pltpu.VMEM((2, rows, points), F32),
            pltpu.VMEM((2, 2, points, 2 * cols), BF16),
            pltpu.VMEM((2, 2, 2 * points, width), BF16),
            pltpu.VMEM((2, 2 * width, 2 * points), BF16),
            pltpu.VMEM((1, rows), F32),
            pltpu.VMEM((1, eps_cond.shape[0]), F32),
            pltpu.VMEM((rows, cols), F32),
            pltpu.VMEM(tile, BF16),
            pltpu.VMEM((2, n_k, 3, rows, cols), BF16),
            pltpu.VMEM((2, n_k, 2, n_val, 1, 2 * width), F32),
            pltpu.VMEM((2, n_k, 2 * n_val, 1, 2 * width), F32),
            pltpu.VMEM((2, n_k, 2) + image, BF16),
            pltpu.VMEM((2, n_k, 4 * n_val) + image, BF16),
            pltpu.VMEM(tile, F32),
            pltpu.VMEM((2, n_k, 2, 3, rows // 2, cols), BF16),
            pltpu.VMEM((2, n_k, 2, 3, rows // 2, cols), BF16),
            pltpu.SemaphoreType.DMA((6,)),
            pltpu.SemaphoreType.DMA((3,)),
            pltpu.SemaphoreType.DMA((3,)),
            pltpu.SemaphoreType.DMA((6,)),
            pltpu.SemaphoreType.DMA((n_k, 6)),
            pltpu.SemaphoreType.REGULAR((2, 2)),
        ],
        compiler_params=pltpu.CompilerParams(
            collective_id=0, has_side_effects=True, vmem_limit_bytes=56 * 1024 * 1024),
    )(trials, psi_val, psi_cond, kernel, eps_val.reshape(1, -1), eps_cond.reshape(1, -1))
    out = jax.ShapeDtypeStruct(tile, F32)
    return pl.pallas_call(
        hand_over,
        out_shape=(out, out),
        in_specs=[hbm, hbm],
        out_specs=(hbm, hbm),
        scratch_shapes=[pltpu.SemaphoreType.DMA((2,))],
        compiler_params=pltpu.CompilerParams(vmem_limit_bytes=1024 * 1024),
    )(*results)


def solution(mesh):
    n_pts, n_val = mesh.shape["pts"], mesh.shape["val"]

    def program(trials, *rest):
        whole_lanes = trials.shape[2] % 128 == 0 and rest[0].shape[1] % 128 == 0
        if whole_lanes and trials.shape[0] == 2 and n_pts == 8 and n_val <= 4:
            return fused(n_pts, n_val, trials, *rest)
        return local(trials, *rest)

    in_specs = (
        P(None, "val", "pts"),
        P("pts", "val"),
        P("pts", None),
        P(None, ("pts", "val")),
        P("val"),
        P(),
    )
    out_specs = (P(None, "val", "pts"), P(None, "val", "pts"))
    return jax.shard_map(program, mesh=mesh, in_specs=in_specs, out_specs=out_specs, check_vma=False)
```

```python
import jax
import jax.numpy as jnp
from jax import lax
from jax.experimental import pallas as pl
from jax.experimental.pallas import tpu as pltpu
from jax.sharding import PartitionSpec as P

center_shift = 1.75
half_width = 1.25


def gathered_inner(local_trial, psi_cond):
    return jnp.einsum(
        "kvc,mc->kvm",
        lax.all_gather(local_trial, "pts", axis=2, tiled=True),
        psi_cond,
        preferred_element_type=jnp.float32,
    )


def orbital_terms(inner, psi_val, psi_cond, kernel):
    rho_part = jnp.einsum("mv,kvm->km", psi_val.astype(jnp.float32), inner)
    rho = lax.psum_scatter(rho_part, "val", scatter_dimension=1, tiled=True).astype(jnp.bfloat16)
    image_part = jnp.einsum("km,nm->kn", rho, kernel, preferred_element_type=jnp.float32)
    image_rows = lax.psum_scatter(
        image_part.astype(jnp.bfloat16), "pts", scatter_dimension=1, tiled=True
    ).astype(jnp.float32)
    image = lax.psum(image_rows, "val")
    weighted = (jnp.transpose(psi_val.astype(jnp.float32))[None] * image[:, None, :]).astype(
        jnp.bfloat16
    )
    return jnp.einsum("kvm,mc->kvc", weighted, psi_cond, preferred_element_type=jnp.float32)


def reduced(partial_sum):
    return lax.psum_scatter(
        partial_sum.astype(jnp.bfloat16), "pts", scatter_dimension=2, tiled=True
    ).astype(jnp.float32)


def local(trials, psi_val, psi_cond, kernel, eps_val, eps_cond):
    cols_own = trials.shape[2]
    index_pts = lax.axis_index("pts")
    diff_whole = (eps_cond[None, :] - eps_val[:, None] - center_shift)[None]
    diff_own = lax.dynamic_slice_in_dim(diff_whole, index_pts * cols_own, cols_own, 2)
    first_image = reduced(
        orbital_terms(gathered_inner(trials, psi_cond), psi_val, psi_cond, kernel)
    )
    first = (diff_own * trials.astype(jnp.float32) + 2.0 * first_image) / half_width
    second_trial = first.astype(jnp.bfloat16)
    second_inner = gathered_inner(second_trial, psi_cond)
    second_image = reduced(orbital_terms(second_inner, psi_val, psi_cond, kernel))
    filtered = 2.0 * (
        diff_own * second_trial.astype(jnp.float32) + 2.0 * second_image
    ) / half_width - trials.astype(jnp.float32)
    return (first, filtered)


F32, BF16 = jnp.float32, jnp.bfloat16
NT = (((1,), (1,)), ((), ()))


def fused_kernel(n_pts, n_val, x_hbm, pv_hbm, pc_hbm, kern_hbm, ev_hbm, ec_hbm, first_ref, filt_ref,
                 x_ref, pv, pvt, cond, kern, kern_t, ev_ref, ec_ref, diff, second, xg, rs, rr, im, ir,
                 acc, part_out, part_in, load_sem, mate_send, mate_recv, send_sem, recv_sem, met_sem):
    p = lax.axis_index("pts")
    z = lax.axis_index("val")
    n_k, rows, cols = x_ref.shape
    pts_own = pv.shape[1]
    width = rr.shape[-1] // 2
    lanes = ir.shape[-1]
    step = 256

    def flipped(q, bit):
        return q + bit - 2 * bit * lax.rem(lax.div(q, bit), 2)

    mate = flipped(p, 1)
    core = lax.rem(p, 2)
    chips = (p, flipped(p, 2), flipped(p, 4), flipped(flipped(p, 2), 4))

    def served(core):
        x_turn, y_turn = flipped(p, 2) - p, flipped(p, 4) - p
        return lax.div(p + y_turn + (1 - core) * x_turn, 2), lax.div(p + core * x_turn, 2)

    barrier = pltpu.get_barrier_semaphore()
    for to in (*chips[1:], mate):
        pl.semaphore_signal(barrier, inc=1, device_id=(to, z), device_id_type=pl.DeviceIdType.MESH)
    below = lax.div(z + n_val - 1, n_val)
    above = lax.div(2 * n_val - 2 - z, n_val)
    sides = ((below, z - below), (above, z + above))
    for there, at in sides:
        @pl.when(there == 1)
        def _():
            for to in (p, mate):
                pl.semaphore_signal(barrier, inc=1, device_id=(to, at), device_id_type=pl.DeviceIdType.MESH)
    load_x = pltpu.make_async_copy(x_hbm, x_ref, load_sem.at[0])
    load_x.start()
    load_pv = pltpu.make_async_copy(pv_hbm, pv.at[0], load_sem.at[1])
    load_pv.start()
    for d in range(4):
        at = pl.multiple_of(chips[d] * cols, cols)
        pltpu.make_async_copy(
            pc_hbm.at[:, pl.ds(at, cols)], cond.at[0, d // 2, :, pl.ds(d % 2 * cols, cols)], load_sem.at[2]).start()
    load_ev = pltpu.make_async_copy(ev_hbm, ev_ref, load_sem.at[3])
    load_ec = pltpu.make_async_copy(ec_hbm, ec_ref, load_sem.at[4])
    load_ev.start()
    load_ec.start()
    load_x.wait()
    pl.semaphore_wait(barrier, 4 + 2 * (below + above))

    def tell(turn):
        for side, (there, at) in enumerate(sides):
            @pl.when(there == 1)
            def _():
                pl.semaphore_signal(met_sem.at[turn, 1 - side], inc=1, device_id=(p, at),
                                    device_id_type=pl.DeviceIdType.MESH)

    def told(turn):
        for side, (there, at) in enumerate(sides):
            @pl.when(there == 1)
            def _():
                pl.semaphore_wait(met_sem.at[turn, side], 1)

    groups = {
        "x_near": lambda it, k: xg.at[it, k, 0],
        "x_far": lambda it, k: xg.at[it, k, 1:3],
        "rho": lambda it, k: rr.at[it, k, 1:2 * n_val],
        "image": lambda it, k: ir.at[it, k],
        "pairs_top": lambda it, k: part_in.at[it, k, 0],
        "pairs_low": lambda it, k: part_in.at[it, k, 1],
    }
    places = {name: at for at, name in enumerate(groups)}

    def wait_for(ref, sem):
        pltpu.make_async_copy(ref, ref, sem).wait()

    def remote(it, k, group, src, dst, to_p, to_z):
        n = places[group]
        pltpu.make_async_remote_copy(
            src_ref=src, dst_ref=dst, send_sem=send_sem.at[n], recv_sem=recv_sem.at[k, n],
            device_id=(to_p, to_z), device_id_type=pl.DeviceIdType.MESH).start()

    def arrived(it, k, group):
        wait_for(groups[group](it, k), recv_sem.at[k, places[group]])

    halves = (("pairs_top", slice(0, rows // 2)), ("pairs_low", slice(rows // 2, rows)))

    def gather_start(it, k, half, x):
        part = halves[half][1]
        for d in (3, 1, 2):
            remote(it, k, "x_near" if d == 1 else "x_far", x.at[k, part], xg.at[it, k, d - 1, part], chips[d], z)

    def to_mate(n, src, dst):
        pltpu.make_async_remote_copy(
            src_ref=src, dst_ref=dst, send_sem=mate_send.at[n], recv_sem=mate_recv.at[n],
            device_id=(mate, z), device_id_type=pl.DeviceIdType.MESH).start()

    def density(it, k, jj, left, right, rho):
        block = jnp.concatenate([left, right], axis=1)
        out = []
        for b in range(2):
            for t in range(pts_own // step):
                zz = lax.dot_general(block, cond[b, jj, t * step:(t + 1) * step, :], NT, preferred_element_type=F32)
                y = zz * pvt[b, :, t * step:(t + 1) * step]
                out.append(jnp.sum(y.reshape(rows // 8, 8, step), axis=0))
        return out if rho is None else [u + w for u, w in zip(rho, out)]

    def rho_start(it, k, rho):
        row = jnp.concatenate([jnp.sum(u, axis=0, keepdims=True) for u in rho], axis=1)
        for s in range(n_val):
            for b in range(2):
                tile = row[:, b * pts_own + s * width:b * pts_own + (s + 1) * width]
                rs[it, k, 0, s, :, b * width:(b + 1) * width] = tile
                rs[it, k, 1, s, :, (1 - b) * width:(2 - b) * width] = tile
        for s in range(n_val - 1, -1, -1):
            to = lax.rem(z + s, n_val)
            for b in range(2):
                if b or s:
                    remote(it, k, "rho", rs.at[it, k, b, to], rr.at[it, k, n_val * b + s], mate if b else p, to)

    def tiled(part):
        sub = lax.broadcasted_iota(jnp.int32, (8, lanes), 0)
        out = part[:, :lanes]
        for i in range(1, pts_own // lanes):
            out = jnp.where(sub == i, part[:, i * lanes:(i + 1) * lanes], out)
        return out

    def image_wait(ref, sem):
        @pl.when(core == 0)
        def _():
            wait_for(ref.at[..., 1:, :, :], sem)

        @pl.when(core == 1)
        def _():
            wait_for(ref, sem)

    def image_start(it, k):
        own = rs[it, k, 0, z]
        arrived(it, k, "rho")
        for i in range(1, 2 * n_val):
            own = own + rr[it, k, i]
        own = jnp.broadcast_to(own, (8, 2 * width)).astype(BF16)
        for j in range(2):
            part = jnp.dot(own, kern_t[j], preferred_element_type=F32)
            part = jnp.concatenate([tiled(part[:, :pts_own]), tiled(part[:, pts_own:])], axis=0).astype(BF16)
            im[it, k, j] = part
            slot = (3 - core) if j == 0 else core
            for s in range(n_val - 1, -1, -1):
                to = lax.rem(z + s, n_val)

                def send(to_core):
                    remote(it, k, "image", im.at[it, k, j], ir.at[it, k, 4 * s + slot],
                           2 * served(core)[j] + to_core, to)

                if s or j == 0:
                    send(0)
                else:
                    @pl.when(core == 0)
                    def _():
                        ir[it, k, 0] = part

                    @pl.when(core == 1)
                    def _():
                        send(0)
                send(1)

    def pairs_start(it, k):
        image_wait(ir.at[it, k], recv_sem.at[k, places["image"]])
        total = ir[it, k, 0].astype(F32)
        for i in range(1, 4 * n_val):
            total = total + ir[it, k, i].astype(F32)
        low, high = total[:8], total[8:]
        images = []
        for b in range(2):
            total = jnp.where(core == b, low, high)
            row = jnp.concatenate([total[i:i + 1] for i in range(pts_own // lanes)], axis=1)
            images.append(row)
        left = [(pvt[b] * images[b]).astype(BF16) for b in range(2)]
        tiles = {}
        for jj in (1, 0):
            both = (jnp.dot(left[0], cond[0, jj], preferred_element_type=F32)
                    + jnp.dot(left[1], cond[1, jj], preferred_element_type=F32))
            for d in ((3, 2), (1, 0))[1 - jj]:
                tile = both[:, d % 2 * cols:(d % 2 + 1) * cols]
                if d == 0:
                    acc[k] = tile
                else:
                    for half, (group, part) in enumerate(halves):
                        part_out[it, k, half, d - 1] = tile[part].astype(BF16)
            if jj == 1:
                for half, (group, part) in enumerate(halves):
                    for d in (3, 2):
                        remote(it, k, group, part_out.at[it, k, half, d - 1], part_in.at[it, k, half, d - 1], chips[d], z)
        for half, (group, part) in enumerate(halves):
            for d in (1,):
                remote(it, k, group, part_out.at[it, k, half, d - 1], part_in.at[it, k, half, d - 1], chips[d], z)

    def pairs_end(it, k, half):
        group, part = halves[half]
        value = acc[k, part]
        arrived(it, k, group)
        for d in (1, 2, 3):
            value = value + part_in[it, k, half, d - 1].astype(F32)
        return value

    def apply(it, x, use):
        every = range(n_k)
        if it == 0:
            for k in every:
                for half in range(2):
                    gather_start(it, k, half, x)
            tell(0)
            to_mate(0, pv_hbm, pv.at[1])
            for d in range(4):
                at = pl.multiple_of(flipped(chips[d], 1) * cols, cols)
                to_mate(1, pc_hbm.at[:, pl.ds(at, cols)], cond.at[1, d // 2, :, pl.ds(d % 2 * cols, cols)])
            for j in range(2):
                part = pl.ds(pl.multiple_of(served(1 - core)[j] * 2 * pts_own, 2 * pts_own), 2 * pts_own)
                to_mate(2, kern_hbm.at[part], kern.at[1, j])
            for j in range(2):
                part = pl.ds(pl.multiple_of(served(core)[j] * 2 * pts_own, 2 * pts_own), 2 * pts_own)
                pltpu.make_async_copy(kern_hbm.at[part], kern.at[0, j], load_sem.at[5]).start()
            load_ev.wait()
            load_ec.wait()
            diff[...] = (ec_ref[:, pl.ds(pl.multiple_of(p * cols, cols), cols)]
                         - jnp.transpose(jnp.broadcast_to(ev_ref[...], (cols, rows))) - center_shift)
            load_pv.wait()
            pvt[0] = jnp.transpose(pv[0].astype(F32))
            told(0)
            tell(1)
            wait_for(pv.at[1], mate_recv.at[0])
            pvt[1] = jnp.transpose(pv[1].astype(F32))
            wait_for(cond.at[0], load_sem.at[2])
            wait_for(cond.at[1], mate_recv.at[1])
        for k in every:
            arrived(it, k, "x_near")
            rho = density(it, k, 0, x[k], xg[it, k, 0], None)
            arrived(it, k, "x_far")
            rho = density(it, k, 1, xg[it, k, 1], xg[it, k, 2], rho)
            if it == 0 and k == 0:
                told(1)
            rho_start(it, k, rho)
        if it == 0:
            for b in range(2):
                wait_for(kern.at[b], mate_recv.at[2] if b else load_sem.at[5])
                for j in range(2):
                    kern_t[j, b * width:(b + 1) * width] = jnp.transpose(kern[b, j])
        for stage in (image_start, pairs_start):
            for k in every:
                stage(it, k)
        if it == 1:
            for n, ref in enumerate((pv.at[1], cond.at[1], kern.at[1])):
                wait_for(ref, mate_send.at[n])
            wait_for(xg.at[:, :, 0], send_sem.at[places["x_near"]])
            wait_for(xg.at[:, :, 1:], send_sem.at[places["x_far"]])
            wait_for(rr.at[:, :, 1:], send_sem.at[places["rho"]])
            image_wait(ir, send_sem.at[places["image"]])
        for k in every:
            for half in range(2):
                use(k, half, pairs_end(it, k, half))

    def to_first(k, half, image):
        part = halves[half][1]
        value = (diff[part] * x_ref[k, part].astype(F32) + 2.0 * image) / half_width
        second[k, part] = value.astype(BF16)
        gather_start(1, k, half, second)
        first_ref[k, part] = value

    def to_filtered(k, half, image):
        part = halves[half][1]
        filt_ref[k, part] = (2.0 * (diff[part] * second[k, part].astype(F32) + 2.0 * image) / half_width
                             - x_ref[k, part].astype(F32))

    apply(0, x_ref, to_first)
    apply(1, second, to_filtered)
    for half, (group, part) in enumerate(halves):
        wait_for(part_in.at[:, :, half], send_sem.at[places[group]])


def hand_over(a, b, a_out, b_out, sem):
    n_k, rows, cols = a.shape
    for k in range(n_k):
        for at in range(0, rows, rows // 4):
            part = slice(at, at + rows // 4)
            pltpu.make_async_copy(a.at[k, part], a_out.at[k, part], sem.at[0]).start()
            pltpu.make_async_copy(b.at[k, part], b_out.at[k, part], sem.at[1]).start()
    pltpu.make_async_copy(a, a_out, sem.at[0]).wait()
    pltpu.make_async_copy(b, b_out, sem.at[1]).wait()


def fused(n_pts, n_val, trials, psi_val, psi_cond, kernel, eps_val, eps_cond):
    n_k, rows, cols = trials.shape
    points = psi_val.shape[0]
    width = kernel.shape[1]
    vmem, hbm = pl.BlockSpec(memory_space=pltpu.VMEM), pl.BlockSpec(memory_space=pl.ANY)
    tile = (n_k, rows, cols)
    image = (2 * points // 128, 128)
    kept = pltpu.VMEM(tile, F32)
    results = pl.pallas_call(
        lambda *refs: fused_kernel(n_pts, n_val, *refs),
        out_shape=(kept, kept),
        in_specs=[hbm] * 6,
        out_specs=(vmem, vmem),
        scratch_shapes=[
            pltpu.VMEM(tile, BF16),
            pltpu.VMEM((2, points, rows), BF16),
            pltpu.VMEM((2, rows, points), F32),
            pltpu.VMEM((2, 2, points, 2 * cols), BF16),
            pltpu.VMEM((2, 2, 2 * points, width), BF16),
            pltpu.VMEM((2, 2 * width, 2 * points), BF16),
            pltpu.VMEM((1, rows), F32),
            pltpu.VMEM((1, eps_cond.shape[0]), F32),
            pltpu.VMEM((rows, cols), F32),
            pltpu.VMEM(tile, BF16),
            pltpu.VMEM((2, n_k, 3, rows, cols), BF16),
            pltpu.VMEM((2, n_k, 2, n_val, 1, 2 * width), F32),
            pltpu.VMEM((2, n_k, 2 * n_val, 1, 2 * width), F32),
            pltpu.VMEM((2, n_k, 2) + image, BF16),
            pltpu.VMEM((2, n_k, 4 * n_val) + image, BF16),
            pltpu.VMEM(tile, F32),
            pltpu.VMEM((2, n_k, 2, 3, rows // 2, cols), BF16),
            pltpu.VMEM((2, n_k, 2, 3, rows // 2, cols), BF16),
            pltpu.SemaphoreType.DMA((6,)),
            pltpu.SemaphoreType.DMA((3,)),
            pltpu.SemaphoreType.DMA((3,)),
            pltpu.SemaphoreType.DMA((6,)),
            pltpu.SemaphoreType.DMA((n_k, 6)),
            pltpu.SemaphoreType.REGULAR((2, 2)),
        ],
        compiler_params=pltpu.CompilerParams(
            collective_id=0, has_side_effects=True, vmem_limit_bytes=56 * 1024 * 1024),
    )(trials, psi_val, psi_cond, kernel, eps_val.reshape(1, -1), eps_cond.reshape(1, -1))
    out = jax.ShapeDtypeStruct(tile, F32)
    return pl.pallas_call(
        hand_over,
        out_shape=(out, out),
        in_specs=[hbm, hbm],
        out_specs=(hbm, hbm),
        scratch_shapes=[pltpu.SemaphoreType.DMA((2,))],
        compiler_params=pltpu.CompilerParams(vmem_limit_bytes=1024 * 1024),
    )(*results)


def solution(mesh):
    n_pts, n_val = mesh.shape["pts"], mesh.shape["val"]

    def program(trials, *rest):
        whole_lanes = trials.shape[2] % 128 == 0 and rest[0].shape[1] % 128 == 0
        if whole_lanes and trials.shape[0] == 2 and n_pts == 8 and n_val <= 4:
            return fused(n_pts, n_val, trials, *rest)
        return local(trials, *rest)

    in_specs = (
        P(None, "val", "pts"),
        P("pts", "val"),
        P("pts", None),
        P(None, ("pts", "val")),
        P("val"),
        P(),
    )
    out_specs = (P(None, "val", "pts"), P(None, "val", "pts"))
    return jax.shard_map(program, mesh=mesh, in_specs=in_specs, out_specs=out_specs, check_vma=False)
```

```python
import jax
import jax.numpy as jnp
from jax import lax
from jax.experimental import pallas as pl
from jax.experimental.pallas import tpu as pltpu
from jax.sharding import PartitionSpec as P

center_shift = 1.75
half_width = 1.25


def gathered_inner(local_trial, psi_cond):
    return jnp.einsum(
        "kvc,mc->kvm",
        lax.all_gather(local_trial, "pts", axis=2, tiled=True),
        psi_cond,
        preferred_element_type=jnp.float32,
    )


def orbital_terms(inner, psi_val, psi_cond, kernel):
    rho_part = jnp.einsum("mv,kvm->km", psi_val.astype(jnp.float32), inner)
    rho = lax.psum_scatter(rho_part, "val", scatter_dimension=1, tiled=True).astype(jnp.bfloat16)
    image_part = jnp.einsum("km,nm->kn", rho, kernel, preferred_element_type=jnp.float32)
    image_rows = lax.psum_scatter(
        image_part.astype(jnp.bfloat16), "pts", scatter_dimension=1, tiled=True
    ).astype(jnp.float32)
    image = lax.psum(image_rows, "val")
    weighted = (jnp.transpose(psi_val.astype(jnp.float32))[None] * image[:, None, :]).astype(
        jnp.bfloat16
    )
    return jnp.einsum("kvm,mc->kvc", weighted, psi_cond, preferred_element_type=jnp.float32)


def reduced(partial_sum):
    return lax.psum_scatter(
        partial_sum.astype(jnp.bfloat16), "pts", scatter_dimension=2, tiled=True
    ).astype(jnp.float32)


def local(trials, psi_val, psi_cond, kernel, eps_val, eps_cond):
    cols_own = trials.shape[2]
    index_pts = lax.axis_index("pts")
    diff_whole = (eps_cond[None, :] - eps_val[:, None] - center_shift)[None]
    diff_own = lax.dynamic_slice_in_dim(diff_whole, index_pts * cols_own, cols_own, 2)
    first_image = reduced(
        orbital_terms(gathered_inner(trials, psi_cond), psi_val, psi_cond, kernel)
    )
    first = (diff_own * trials.astype(jnp.float32) + 2.0 * first_image) / half_width
    second_trial = first.astype(jnp.bfloat16)
    second_inner = gathered_inner(second_trial, psi_cond)
    second_image = reduced(orbital_terms(second_inner, psi_val, psi_cond, kernel))
    filtered = 2.0 * (
        diff_own * second_trial.astype(jnp.float32) + 2.0 * second_image
    ) / half_width - trials.astype(jnp.float32)
    return (first, filtered)


F32, BF16 = jnp.float32, jnp.bfloat16
NT = (((1,), (1,)), ((), ()))


def fused_kernel(n_pts, n_val, x_hbm, pv_hbm, pc_hbm, kern_hbm, ev_hbm, ec_hbm, first_ref, filt_ref,
                 x_ref, pv, pvt, cond, kern, kern_t, ev_ref, ec_ref, diff, second, xg, rs, rr, im, ir,
                 acc, part_out, part_in, load_sem, mate_send, mate_recv, send_sem, recv_sem, met_sem):
    p = lax.axis_index("pts")
    z = lax.axis_index("val")
    n_k, rows, cols = x_ref.shape
    pts_own = pv.shape[1]
    width = rr.shape[-1] // 2
    lanes = ir.shape[-1]
    step = 256

    def flipped(q, bit):
        return q + bit - 2 * bit * lax.rem(lax.div(q, bit), 2)

    mate = flipped(p, 1)
    core = lax.rem(p, 2)
    chips = (p, flipped(p, 2), flipped(p, 4), flipped(flipped(p, 2), 4))

    def served(core):
        x_turn, y_turn = flipped(p, 2) - p, flipped(p, 4) - p
        return lax.div(p + y_turn + (1 - core) * x_turn, 2), lax.div(p + core * x_turn, 2)

    barrier = pltpu.get_barrier_semaphore()
    for to in (*chips[1:], mate):
        pl.semaphore_signal(barrier, inc=1, device_id=(to, z), device_id_type=pl.DeviceIdType.MESH)
    below = lax.div(z + n_val - 1, n_val)
    above = lax.div(2 * n_val - 2 - z, n_val)
    sides = ((below, z - below), (above, z + above))
    for there, at in sides:
        @pl.when(there == 1)
        def _():
            for to in (p, mate):
                pl.semaphore_signal(barrier, inc=1, device_id=(to, at), device_id_type=pl.DeviceIdType.MESH)
    load_x = pltpu.make_async_copy(x_hbm, x_ref, load_sem.at[0])
    load_x.start()
    load_pv = pltpu.make_async_copy(pv_hbm, pv.at[0], load_sem.at[1])
    load_pv.start()
    for d in range(4):
        at = pl.multiple_of(chips[d] * cols, cols)
        pltpu.make_async_copy(
            pc_hbm.at[:, pl.ds(at, cols)], cond.at[0, d // 2, :, pl.ds(d % 2 * cols, cols)], load_sem.at[2]).start()
    load_ev = pltpu.make_async_copy(ev_hbm, ev_ref, load_sem.at[3])
    load_ec = pltpu.make_async_copy(ec_hbm, ec_ref, load_sem.at[4])
    load_ev.start()
    load_ec.start()
    load_x.wait()
    pl.semaphore_wait(barrier, 4 + 2 * (below + above))

    def tell(turn):
        for side, (there, at) in enumerate(sides):
            @pl.when(there == 1)
            def _():
                pl.semaphore_signal(met_sem.at[turn, 1 - side], inc=1, device_id=(p, at),
                                    device_id_type=pl.DeviceIdType.MESH)

    def told(turn):
        for side, (there, at) in enumerate(sides):
            @pl.when(there == 1)
            def _():
                pl.semaphore_wait(met_sem.at[turn, side], 1)

    groups = {
        "near_top": lambda it, k: xg.at[it, k, 0, :rows // 2],
        "far_top": lambda it, k: xg.at[it, k, 1:3, :rows // 2],
        "near_low": lambda it, k: xg.at[it, k, 0, rows // 2:],
        "far_low": lambda it, k: xg.at[it, k, 1:3, rows // 2:],
        "rho": lambda it, k: rr.at[it, k, 1:2 * n_val],
        "image": lambda it, k: ir.at[it, k],
        "pairs_top": lambda it, k: part_in.at[it, k, 0],
        "pairs_low": lambda it, k: part_in.at[it, k, 1],
    }
    places = {name: at for at, name in enumerate(groups)}

    def wait_for(ref, sem):
        pltpu.make_async_copy(ref, ref, sem).wait()

    def remote(it, k, group, src, dst, to_p, to_z):
        n = places[group]
        pltpu.make_async_remote_copy(
            src_ref=src, dst_ref=dst, send_sem=send_sem.at[n], recv_sem=recv_sem.at[k, n],
            device_id=(to_p, to_z), device_id_type=pl.DeviceIdType.MESH).start()

    def arrived(it, k, group):
        wait_for(groups[group](it, k), recv_sem.at[k, places[group]])

    halves = (("pairs_top", slice(0, rows // 2)), ("pairs_low", slice(rows // 2, rows)))

    def gather_start(it, k, half, x):
        part = halves[half][1]
        for d in (3, 1, 2):
            remote(it, k, (("near_top", "far_top"), ("near_low", "far_low"))[half][d != 1], x.at[k, part], xg.at[it, k, d - 1, part], chips[d], z)

    def to_mate(n, src, dst):
        pltpu.make_async_remote_copy(
            src_ref=src, dst_ref=dst, send_sem=mate_send.at[n], recv_sem=mate_recv.at[n],
            device_id=(mate, z), device_id_type=pl.DeviceIdType.MESH).start()

    def density(jj, part, left, right, rho):
        block = jnp.concatenate([left, right], axis=1)
        out = []
        for b in range(2):
            for t in range(pts_own // step):
                zz = lax.dot_general(block, cond[b, jj, t * step:(t + 1) * step, :], NT, preferred_element_type=F32)
                y = zz * pvt[b, part, t * step:(t + 1) * step]
                out.append(jnp.sum(y.reshape(-1, 8, step), axis=0))
        return out if rho is None else [u + w for u, w in zip(rho, out)]

    def rho_start(it, k, rho):
        row = jnp.concatenate([jnp.sum(u, axis=0, keepdims=True) for u in rho], axis=1)
        for s in range(n_val):
            for b in range(2):
                tile = row[:, b * pts_own + s * width:b * pts_own + (s + 1) * width]
                rs[it, k, 0, s, :, b * width:(b + 1) * width] = tile
                rs[it, k, 1, s, :, (1 - b) * width:(2 - b) * width] = tile
        for s in range(n_val - 1, -1, -1):
            to = lax.rem(z + s, n_val)
            for b in range(2):
                if b or s:
                    remote(it, k, "rho", rs.at[it, k, b, to], rr.at[it, k, n_val * b + s], mate if b else p, to)

    def tiled(part):
        sub = lax.broadcasted_iota(jnp.int32, (8, lanes), 0)
        out = part[:, :lanes]
        for i in range(1, pts_own // lanes):
            out = jnp.where(sub == i, part[:, i * lanes:(i + 1) * lanes], out)
        return out

    def image_wait(ref, sem):
        @pl.when(core == 0)
        def _():
            wait_for(ref.at[..., 1:, :, :], sem)

        @pl.when(core == 1)
        def _():
            wait_for(ref, sem)

    def image_start(it, k):
        own = rs[it, k, 0, z]
        arrived(it, k, "rho")
        for i in range(1, 2 * n_val):
            own = own + rr[it, k, i]
        own = jnp.broadcast_to(own, (8, 2 * width)).astype(BF16)
        for j in range(2):
            blocks = [jnp.dot(own, kern_t[j, :, b * pts_own:(b + 1) * pts_own], preferred_element_type=F32)
                      for b in range(2)]
            part = jnp.concatenate([tiled(block) for block in blocks], axis=0).astype(BF16)
            im[it, k, j] = part
            slot = (3 - core) if j == 0 else core
            for s in range(n_val - 1, -1, -1):
                to = lax.rem(z + s, n_val)

                def send(to_core):
                    remote(it, k, "image", im.at[it, k, j], ir.at[it, k, 4 * s + slot],
                           2 * served(core)[j] + to_core, to)

                if s or j == 0:
                    send(0)
                else:
                    @pl.when(core == 0)
                    def _():
                        ir[it, k, 0] = part

                    @pl.when(core == 1)
                    def _():
                        send(0)
                send(1)

    def pairs_start(it, k):
        image_wait(ir.at[it, k], recv_sem.at[k, places["image"]])
        total = ir[it, k, 0].astype(F32)
        for i in range(1, 4 * n_val):
            total = total + ir[it, k, i].astype(F32)
        low, high = total[:8], total[8:]
        images = []
        for b in range(2):
            total = jnp.where(core == b, low, high)
            row = jnp.concatenate([total[i:i + 1] for i in range(pts_own // lanes)], axis=1)
            images.append(row)
        left = [(pvt[b] * images[b]).astype(BF16) for b in range(2)]
        tiles = {}
        for jj in (1, 0):
            both = (jnp.dot(left[0], cond[0, jj], preferred_element_type=F32)
                    + jnp.dot(left[1], cond[1, jj], preferred_element_type=F32))
            for d in ((3, 2), (1, 0))[1 - jj]:
                tile = both[:, d % 2 * cols:(d % 2 + 1) * cols]
                if d == 0:
                    acc[k] = tile
                else:
                    for half, (group, part) in enumerate(halves):
                        part_out[it, k, half, d - 1] = tile[part].astype(BF16)
            if jj == 1:
                for half, (group, part) in enumerate(halves):
                    for d in (3, 2):
                        remote(it, k, group, part_out.at[it, k, half, d - 1], part_in.at[it, k, half, d - 1], chips[d], z)
        for half, (group, part) in enumerate(halves):
            for d in (1,):
                remote(it, k, group, part_out.at[it, k, half, d - 1], part_in.at[it, k, half, d - 1], chips[d], z)

    def pairs_end(it, k, half):
        group, part = halves[half]
        value = acc[k, part]
        arrived(it, k, group)
        for d in (1, 2, 3):
            value = value + part_in[it, k, half, d - 1].astype(F32)
        return value

    def apply(it, x, use):
        every = range(n_k)
        if it == 0:
            for k in every:
                for half in range(2):
                    gather_start(it, k, half, x)
            tell(0)
            to_mate(0, pv_hbm, pv.at[1])
            for d in range(4):
                at = pl.multiple_of(flipped(chips[d], 1) * cols, cols)
                to_mate(1, pc_hbm.at[:, pl.ds(at, cols)], cond.at[1, d // 2, :, pl.ds(d % 2 * cols, cols)])
            for j in range(2):
                part = pl.ds(pl.multiple_of(served(1 - core)[j] * 2 * pts_own, 2 * pts_own), 2 * pts_own)
                to_mate(2, kern_hbm.at[part], kern.at[1, j])
            for j in range(2):
                part = pl.ds(pl.multiple_of(served(core)[j] * 2 * pts_own, 2 * pts_own), 2 * pts_own)
                pltpu.make_async_copy(kern_hbm.at[part], kern.at[0, j], load_sem.at[5]).start()
            load_ev.wait()
            load_ec.wait()
            diff[...] = (ec_ref[:, pl.ds(pl.multiple_of(p * cols, cols), cols)]
                         - jnp.transpose(jnp.broadcast_to(ev_ref[...], (cols, rows))) - center_shift)
            load_pv.wait()
            pvt[0] = jnp.transpose(pv[0].astype(F32))
            told(0)
            tell(1)
            wait_for(pv.at[1], mate_recv.at[0])
            pvt[1] = jnp.transpose(pv[1].astype(F32))
            wait_for(cond.at[0], load_sem.at[2])
            wait_for(cond.at[1], mate_recv.at[1])
        for k in every:
            rho = None
            for (near, far), (group, part) in zip((("near_top", "far_top"), ("near_low", "far_low")), halves):
                arrived(it, k, near)
                rho = density(0, part, x[k, part], xg[it, k, 0, part], rho)
                arrived(it, k, far)
                rho = density(1, part, xg[it, k, 1, part], xg[it, k, 2, part], rho)
            if it == 0 and k == 0:
                told(1)
            rho_start(it, k, rho)
        if it == 0:
            for b in range(2):
                wait_for(kern.at[b], mate_recv.at[2] if b else load_sem.at[5])
                for j in range(2):
                    kern_t[j, b * width:(b + 1) * width] = jnp.transpose(kern[b, j])
        for stage in (image_start, pairs_start):
            for k in every:
                stage(it, k)
        if it == 1:
            for n, ref in enumerate((pv.at[1], cond.at[1], kern.at[1])):
                wait_for(ref, mate_send.at[n])
            for half, (near, far) in enumerate((("near_top", "far_top"), ("near_low", "far_low"))):
                part = halves[half][1]
                wait_for(xg.at[:, :, 0, part], send_sem.at[places[near]])
                wait_for(xg.at[:, :, 1:, part], send_sem.at[places[far]])
            wait_for(rr.at[:, :, 1:], send_sem.at[places["rho"]])
            image_wait(ir, send_sem.at[places["image"]])
        for k in every:
            for half in range(2):
                use(k, half, pairs_end(it, k, half))

    def to_first(k, half, image):
        part = halves[half][1]
        value = (diff[part] * x_ref[k, part].astype(F32) + 2.0 * image) / half_width
        second[k, part] = value.astype(BF16)
        gather_start(1, k, half, second)
        first_ref[k, part] = value

    def to_filtered(k, half, image):
        part = halves[half][1]
        filt_ref[k, part] = (2.0 * (diff[part] * second[k, part].astype(F32) + 2.0 * image) / half_width
                             - x_ref[k, part].astype(F32))

    apply(0, x_ref, to_first)
    apply(1, second, to_filtered)
    for half, (group, part) in enumerate(halves):
        wait_for(part_in.at[:, :, half], send_sem.at[places[group]])


def hand_over(a, b, a_out, b_out, sem):
    n_k, rows, cols = a.shape
    for k in range(n_k):
        for at in range(0, rows, rows // 4):
            part = slice(at, at + rows // 4)
            pltpu.make_async_copy(a.at[k, part], a_out.at[k, part], sem.at[0]).start()
            pltpu.make_async_copy(b.at[k, part], b_out.at[k, part], sem.at[1]).start()
    pltpu.make_async_copy(a, a_out, sem.at[0]).wait()
    pltpu.make_async_copy(b, b_out, sem.at[1]).wait()


def fused(n_pts, n_val, trials, psi_val, psi_cond, kernel, eps_val, eps_cond):
    n_k, rows, cols = trials.shape
    points = psi_val.shape[0]
    width = kernel.shape[1]
    vmem, hbm = pl.BlockSpec(memory_space=pltpu.VMEM), pl.BlockSpec(memory_space=pl.ANY)
    tile = (n_k, rows, cols)
    image = (2 * points // 128, 128)
    kept = pltpu.VMEM(tile, F32)
    results = pl.pallas_call(
        lambda *refs: fused_kernel(n_pts, n_val, *refs),
        out_shape=(kept, kept),
        in_specs=[hbm] * 6,
        out_specs=(vmem, vmem),
        scratch_shapes=[
            pltpu.VMEM(tile, BF16),
            pltpu.VMEM((2, points, rows), BF16),
            pltpu.VMEM((2, rows, points), F32),
            pltpu.VMEM((2, 2, points, 2 * cols), BF16),
            pltpu.VMEM((2, 2, 2 * points, width), BF16),
            pltpu.VMEM((2, 2 * width, 2 * points), BF16),
            pltpu.VMEM((1, rows), F32),
            pltpu.VMEM((1, eps_cond.shape[0]), F32),
            pltpu.VMEM((rows, cols), F32),
            pltpu.VMEM(tile, BF16),
            pltpu.VMEM((2, n_k, 3, rows, cols), BF16),
            pltpu.VMEM((2, n_k, 2, n_val, 1, 2 * width), F32),
            pltpu.VMEM((2, n_k, 2 * n_val, 1, 2 * width), F32),
            pltpu.VMEM((2, n_k, 2) + image, BF16),
            pltpu.VMEM((2, n_k, 4 * n_val) + image, BF16),
            pltpu.VMEM(tile, F32),
            pltpu.VMEM((2, n_k, 2, 3, rows // 2, cols), BF16),
            pltpu.VMEM((2, n_k, 2, 3, rows // 2, cols), BF16),
            pltpu.SemaphoreType.DMA((6,)),
            pltpu.SemaphoreType.DMA((3,)),
            pltpu.SemaphoreType.DMA((3,)),
            pltpu.SemaphoreType.DMA((8,)),
            pltpu.SemaphoreType.DMA((n_k, 8)),
            pltpu.SemaphoreType.REGULAR((2, 2)),
        ],
        compiler_params=pltpu.CompilerParams(
            collective_id=0, has_side_effects=True, vmem_limit_bytes=56 * 1024 * 1024),
    )(trials, psi_val, psi_cond, kernel, eps_val.reshape(1, -1), eps_cond.reshape(1, -1))
    out = jax.ShapeDtypeStruct(tile, F32)
    return pl.pallas_call(
        hand_over,
        out_shape=(out, out),
        in_specs=[hbm, hbm],
        out_specs=(hbm, hbm),
        scratch_shapes=[pltpu.SemaphoreType.DMA((2,))],
        compiler_params=pltpu.CompilerParams(vmem_limit_bytes=1024 * 1024),
    )(*results)


def solution(mesh):
    n_pts, n_val = mesh.shape["pts"], mesh.shape["val"]

    def program(trials, *rest):
        whole_lanes = trials.shape[2] % 128 == 0 and rest[0].shape[1] % 128 == 0
        if whole_lanes and trials.shape[0] == 2 and n_pts == 8 and n_val <= 4:
            return fused(n_pts, n_val, trials, *rest)
        return local(trials, *rest)

    in_specs = (
        P(None, "val", "pts"),
        P("pts", "val"),
        P("pts", None),
        P(None, ("pts", "val")),
        P("val"),
        P(),
    )
    out_specs = (P(None, "val", "pts"), P(None, "val", "pts"))
    return jax.shard_map(program, mesh=mesh, in_specs=in_specs, out_specs=out_specs, check_vma=False)
```
